512 devices in a mesh: bead: 32 (over x, z_lo), space: 16 (over y, z_hi, core).
Axes of the slice: x: 4, y: 4, z: 16 (z_hi: 2, z_lo: 8; z = z_hi * 8 + z_lo), core: 2. Of those that a mesh axis runs over, the one named last changes fastest.
Arguments:
- positions: float32 [32, 256, 3, 128], P('bead', 'space'), may hold values from 0 to 1
- momenta: float32 [32, 256, 3, 128], P('bead', 'space'), may hold values from -3 to 3
- noise: float32 [32, 256, 3, 128], P('bead', 'space'), may hold values from -6 to 6
- atom_types: int32 [256, 128], P('space'), may hold values from 0 to 3
- occupancy: int32 [256], P('space'), may hold values from 64 to 128, as said below
- type_sigma: float32 [4], replicated, may hold values from 0.2 to 0.4
- type_eps: float32 [4], replicated, may hold values from 0.5 to 2
- type_mass: float32 [4], replicated, may hold values from 1 to 4
Outputs:
- new_positions: float32 [32, 256, 3, 128], P('bead', 'space')
- new_momenta: float32 [32, 256, 3, 128], P('bead', 'space')
The draws below stay inside these ranges and needn't reach their ends.
Inputs may be any that keep to these rules, and one draw needn't show every extreme that they name: `occupancy`: in each domain of 16 consecutive cells some cell holds 128 atoms.
All inputs are finite; a program needn't handle non-finite values.
Results may differ from the reference program's by a relative error of at most 0.0002.
Values sent between devices are 32-bit elements; how exact they have to be, the bound alone decides.
A program may use at most 64 MiB of HBM per device.

```python
import math
import jax
import jax.numpy as jnp
from jax import lax

P_SIZE = 32
PC = 8
A = 128
NTYPES = 4
GY = 4
GZ = 4
CELLS_ALL = 256
N_SPACE = 16


def draw_occupancy(key, part):
    per_domain = GY * GZ
    counts = jax.random.randint(jax.random.fold_in(key, 21), (CELLS_ALL,), A // 2, A + 1)
    fullest = jax.random.randint(jax.random.fold_in(key, 22), (CELLS_ALL // per_domain,), 0, per_domain)
    marked = jnp.arange(CELLS_ALL) % per_domain == jnp.repeat(fullest, per_domain)
    return jnp.where(marked, A, counts).astype(jnp.int32)


def with_ends(values, key, smallest, top_value):
    longest = values.shape.index(max(values.shape))
    spots = []
    for shift in (0, 1):
        where = [jax.random.randint(jax.random.fold_in(key, axis), (), 0, length) for axis, length in enumerate(values.shape)]
        where[longest] = (where[longest] + shift) % values.shape[longest]
        spots.append(tuple(where))
    return values.at[spots[0]].set(smallest).at[spots[1]].set(top_value)


def shard_levels(stream_key, dims, split, smallest, top_value):
    def one(position, parts):
        steps = jax.random.uniform(jax.random.fold_in(jax.random.fold_in(stream_key, 6), position), (parts,), jnp.float32, smallest / len(split), top_value / len(split))
        return jnp.repeat(jnp.exp(steps), dims[position] // parts).reshape((-1,) + (1,) * (len(dims) - position - 1))

    factor_of = one(*split[0])
    for cut in split[1:]:
        factor_of = factor_of * one(*cut)
    return factor_of


def gaussian(rng, shape, spread, most, pieces=(), kind=jnp.bfloat16):
    entries = jax.random.normal(rng, shape, jnp.float32) * spread
    if len(pieces) > 0:
        entries = shard_levels(rng, shape, pieces, -0.22, 0.18) * entries
    return jnp.clip(entries, min=-most, max=most).astype(kind)


def setup_inputs(seed: int = 0) -> dict:
    splits = jax.random.split(jax.random.key(seed), 9)
    positions = jnp.clip(1.0 * jax.random.uniform(splits[0], (P_SIZE, CELLS_ALL, 3, A), jnp.float32) ** shard_levels(splits[0], (P_SIZE, CELLS_ALL, 3, A), ((0, 32), (1, 16)), -0.2, 0.2), 0.0, 1.0)
    momenta = gaussian(splits[1], (P_SIZE, CELLS_ALL, 3, A), 0.5, 3.0, ((0, 32), (1, 16)), jnp.float32)
    noise = gaussian(splits[2], (P_SIZE, CELLS_ALL, 3, A), 1.0, 6.0, ((0, 32), (1, 16)), jnp.float32)
    atom_types = with_ends(jax.random.randint(splits[3], (CELLS_ALL, A), 0, NTYPES), jax.random.fold_in(splits[3], 1), 0, NTYPES - 1).astype(jnp.int32)
    occupancy = draw_occupancy(jax.random.fold_in(splits[8], 71), 0)
    type_sigma = jnp.clip(jax.random.uniform(splits[5], (NTYPES,), jnp.float32, 0.2, 0.4), 0.2, 0.4)
    type_eps = jnp.clip(jnp.exp(jax.random.uniform(splits[6], (NTYPES,), jnp.float32, math.log(0.5), math.log(2.0))), 0.5, 2.0)
    type_mass = jnp.clip(jnp.exp(jax.random.uniform(splits[7], (NTYPES,), jnp.float32, math.log(1.0), math.log(4.0))), 1.0, 4.0)
    return dict(positions=positions, momenta=momenta, noise=noise, atom_types=atom_types, occupancy=occupancy, type_sigma=type_sigma, type_eps=type_eps, type_mass=type_mass)


TIME_STEP = 0.05
INVERSE_TEMP = 32.0
CENTROID_FRICTION = 1.0
INNER_CUT = 0.5
OUTER_CUT = 1.0
precise = lax.Precision.HIGHEST

def stencil_table(cell_total, per_domain, depth_z, height_y):
    in_domain = jnp.arange(cell_total) % per_domain
    across = in_domain // depth_z
    upward = in_domain % depth_z
    offsets = jnp.arange(27)
    step_x = offsets // 9 - 1
    step_y = offsets // 3 % 3 - 1
    step_z = offsets % 3 - 1
    target_y = across[:, None] + step_y[None, :]
    target_z = upward[:, None] + step_z[None, :]
    inside = (target_y >= 0) & (target_y < height_y) & (target_z >= 0) & (target_z < depth_z)
    entry = (step_x[None, :] + 1) * per_domain + target_y * depth_z + target_z
    return jnp.where(inside, entry, 3 * per_domain).astype(jnp.int32)

def mode_table(number):
    bead_rows = jnp.arange(number, dtype=jnp.float32)[:, None]
    column = jnp.arange(number, dtype=jnp.float32)[None, :]
    phases = 2.0 * jnp.pi * bead_rows * column / number
    factor = jnp.sqrt(2.0 / number)
    middle = jnp.cos(jnp.pi * bead_rows) / jnp.sqrt(float(number))
    matrix = jnp.where(column < number / 2, factor * jnp.cos(phases), factor * jnp.sin(phases))
    matrix = jnp.where(column == number / 2, middle, matrix)
    matrix = jnp.where(column == 0, 1.0 / jnp.sqrt(float(number)), matrix)
    return matrix.astype(jnp.float32)

def contract_table(full_count, reduced):
    selected = jnp.arange(reduced)
    selected = jnp.where(selected <= reduced // 2, selected, selected + full_count - reduced)
    chosen = mode_table(full_count)[:, selected]
    product = jnp.dot(mode_table(reduced), chosen.T, precision=precise, preferred_element_type=jnp.float32)
    return jnp.sqrt(reduced / full_count) * product

def propagate(position_modes, momentum_modes, noise_modes):
    number = position_modes.shape[0]
    mode_index = jnp.arange(number)
    frequency = 2.0 * (number / INVERSE_TEMP) * jnp.sin(jnp.pi * mode_index.astype(jnp.float32) / number)
    friction = jnp.where(mode_index == 0, CENTROID_FRICTION, 2.0 * frequency)
    damping = jnp.exp(-friction * TIME_STEP)
    kicking = jnp.sqrt((1.0 - damping * damping) / INVERSE_TEMP)
    cosine = jnp.cos(frequency * TIME_STEP)
    sine_term = jnp.sin(frequency * TIME_STEP)
    drift_factor = jnp.where(mode_index == 0, TIME_STEP, sine_term / jnp.where(mode_index == 0, 1.0, frequency))
    spring = frequency * sine_term
    trailing = (number,) + (1,) * (position_modes.ndim - 1)
    damping = damping.reshape(trailing)
    kicking = kicking.reshape(trailing)
    cosine = cosine.reshape(trailing)
    drift_factor = drift_factor.reshape(trailing)
    spring = spring.reshape(trailing)
    momentum = damping * momentum_modes + kicking * noise_modes
    next_position = cosine * position_modes + drift_factor * momentum
    next_momentum = cosine * momentum - spring * position_modes
    return (next_position, next_momentum)

def atom_table(atom_types, occupancy, type_sigma, type_eps, type_mass):
    type_codes = jnp.arange(type_sigma.shape[0])
    onehot = (atom_types[..., None] == type_codes).astype(jnp.float32)
    sigma_atom = lax.optimization_barrier(jnp.sum(onehot * type_sigma, -1))
    energy_root = jnp.sqrt(lax.optimization_barrier(jnp.sum(onehot * type_eps, -1)))
    mass_atom = lax.optimization_barrier(jnp.sum(onehot * type_mass, -1))
    slot_index = jnp.arange(atom_types.shape[-1])
    living = (slot_index[None, :] < occupancy[:, None]).astype(jnp.float32)
    return (jnp.stack([sigma_atom, energy_root, living], 1), mass_atom)

def anchor_of(ext_index, domain_cells, slab_depth):
    slab_layer = ext_index // domain_cells - 1
    within = ext_index % domain_cells
    return jnp.stack([slab_layer, within // slab_depth, within % slab_depth], -1).astype(jnp.float32)

def taper(radius_sq, cutoff):
    margin = jnp.maximum(0.0, 1.0 - radius_sq / (cutoff * cutoff))
    return (margin * margin, -2.0 * margin / (cutoff * cutoff))

def pair_force(left_position, left_param, right_position, right_param, longer):
    separation = left_position[:, :, None] - right_position[:, None, :]
    radius_sq = lax.optimization_barrier(jnp.sum(separation * separation, 0))
    sigma_pair = 0.5 * (left_param[0][:, None] + right_param[0][None, :])
    sigma_sq = sigma_pair * sigma_pair
    energy = left_param[1][:, None] * right_param[1][None, :]
    shifted = radius_sq + sigma_sq
    quotient = sigma_sq / shifted
    sixth_power = quotient * quotient * quotient
    potential = 4.0 * energy * (sixth_power * sixth_power - sixth_power)
    derivative = -12.0 * energy * (2.0 * sixth_power - 1.0) * sixth_power / shifted
    outer_value, outer_slope = taper(radius_sq, OUTER_CUT)
    inner_value, inner_slope = taper(radius_sq, INNER_CUT)
    if longer:
        switch = outer_value - inner_value
        switch_slope = outer_slope - inner_slope
    else:
        switch = inner_value
        switch_slope = inner_slope
    weight = -2.0 * (derivative * switch + potential * switch_slope)
    weight = weight * left_param[2][:, None] * right_param[2][None, :]
    return lax.optimization_barrier(jnp.sum(weight[None] * separation, 2))

def reference(positions, momenta, noise, atom_types, occupancy, type_sigma, type_eps, type_mass):
    total_beads = positions.shape[0]
    all_cells = positions.shape[1]
    domain_cells = GY * GZ
    neighbours = stencil_table(all_cells, domain_cells, GZ, GY)
    params, mass_atom = atom_table(atom_types, occupancy, type_sigma, type_eps, type_mass)
    root_mass = jnp.sqrt(mass_atom)[None, :, None, :]
    domain = jnp.arange(all_cells) // domain_cells
    within = jnp.arange(all_cells) % domain_cells
    missing = neighbours == 3 * domain_cells
    source = (domain[:, None] + neighbours // domain_cells - 1) % N_SPACE * domain_cells + neighbours % domain_cells
    source = jnp.where(missing, all_cells, source).astype(jnp.int32)
    right_anchor = anchor_of(neighbours, domain_cells, GZ)
    left_anchor = anchor_of(within + domain_cells, domain_cells, GZ)
    param_padded = jnp.concatenate([params, jnp.zeros_like(params[:1])], 0)

    def field(coords, longer):
        padded = jnp.concatenate([coords, jnp.zeros_like(coords[:, :1])], 1)
        bead_total = coords.shape[0]

        def one_cell(cell_index):
            listing = source[cell_index]
            left_all = coords[:, cell_index] + left_anchor[cell_index][None, :, None]
            right_all = padded[:, listing] + right_anchor[cell_index][None, :, :, None]
            right_all = jnp.transpose(right_all, (0, 2, 1, 3)).reshape(bead_total, 3, -1)
            right_param = jnp.transpose(param_padded[listing], (1, 0, 2)).reshape(3, -1)
            left_param = params[cell_index]

            def per_bead(left_position, right_position):
                return pair_force(left_position, left_param, right_position, right_param, longer)
            return jax.vmap(per_bead)(left_all, right_all)
        result = lax.map(one_cell, jnp.arange(all_cells))
        return jnp.transpose(result, (1, 0, 2, 3))
    short_force = field(positions, False)
    kicked = momenta + 0.5 * TIME_STEP * short_force
    matrix = mode_table(total_beads)
    position_modes = jnp.einsum('kn,kcda->ncda', matrix, positions * root_mass, precision=precise)
    momentum_modes = jnp.einsum('kn,kcda->ncda', matrix, kicked / root_mass, precision=precise)
    noise_modes = jnp.einsum('kn,kcda->ncda', matrix, noise, precision=precise)
    moved_position, moved_momentum = propagate(position_modes, momentum_modes, noise_modes)
    new_positions = jnp.einsum('kn,ncda->kcda', matrix, moved_position, precision=precise) / root_mass
    free_momenta = jnp.einsum('kn,ncda->kcda', matrix, moved_momentum, precision=precise) * root_mass
    weights = contract_table(total_beads, PC)
    contracted = jnp.einsum('rk,kcda->rcda', weights, new_positions, precision=precise)
    slow_force = field(contracted, True)
    spread_force = total_beads / PC * jnp.einsum('rk,rcda->kcda', weights, slow_force, precision=precise)
    new_momenta = free_momenta + 0.5 * TIME_STEP * spread_force
    return (new_positions, new_momenta)
```

```python
import functools
import math

import jax
import jax.numpy as jnp
import numpy as np
from jax import lax
from jax.experimental import pallas as pl
from jax.experimental.pallas import tpu as pltpu
from jax.sharding import PartitionSpec as P

F32 = jnp.float32
MESH = pl.DeviceIdType.MESH
NB = 32
NS = 16
PC = 8
TIME_STEP = 0.05
INVERSE_TEMP = 32.0
CENTROID_FRICTION = 1.0


def mode_table(n):
    k = np.arange(n)[:, None].astype(np.float64)
    m = np.arange(n)[None, :].astype(np.float64)
    phase = 2.0 * np.pi * k * m / n
    c = np.where(m < n / 2, np.sqrt(2.0 / n) * np.cos(phase), np.sqrt(2.0 / n) * np.sin(phase))
    c = np.where(m == n / 2, np.cos(np.pi * k) / np.sqrt(n), c)
    return np.where(m == 0, 1.0 / np.sqrt(n), c)


def bead_tables():
    c = mode_table(NB)
    n = np.arange(NB)
    freq = 2.0 * (NB / INVERSE_TEMP) * np.sin(np.pi * n / NB)
    gamma = np.where(n == 0, CENTROID_FRICTION, 2.0 * freq)
    c1 = np.exp(-gamma * TIME_STEP)
    kick = np.sqrt((1.0 - c1 * c1) / INVERSE_TEMP)
    cosine = np.cos(freq * TIME_STEP)
    sine = np.sin(freq * TIME_STEP)
    drift = np.where(n == 0, TIME_STEP, sine / np.where(n == 0, 1.0, freq))

    def mix(d):
        return (c * d[None, :]) @ c.T

    pick = np.arange(PC)
    pick = np.where(pick <= PC // 2, pick, pick + NB - PC)
    w = np.sqrt(PC / NB) * mode_table(PC) @ c[:, pick].T
    x_from = (mix(cosine), mix(drift * kick), mix(drift * c1))
    p_from = (mix(-freq * sine), mix(cosine * kick), mix(cosine * c1))
    early_x = np.concatenate([x_from[0], p_from[0], w @ x_from[0]], 0)
    early_n = np.concatenate([x_from[1], p_from[1], w @ x_from[1]], 0)
    late = np.concatenate([x_from[2], p_from[2], w @ x_from[2]], 0)
    table = np.concatenate([early_x, early_n, late], 0).astype(np.float32)
    weights = (w * (0.5 * TIME_STEP * NB / PC)).astype(np.float32)
    return table, weights


def share_bead(cell):
    return (cell // 4) * 8 + 2 + cell % 4


def kernel(own_ref, early_ref, aux_ref, table_ref, w_ref, nx_ref, np_ref,
           ext, xi, acc, eb, kb, late_out, mixed, cont, ret, rb, cb, xs, sacc, fb, xb, zs, zb,
           halo_ss, halo_rs, early_ss, early_rs, late_ss, late_rs, cont_ss, cont_rs, ret_ss, ret_rs,
           xb_ss, xb_rs, zb_ss, zb_rs):
    b = lax.axis_index("bead")
    s = lax.axis_index("space")
    bx = b // 8
    bz8 = b % 8
    up = (s + 1) % NS
    down = (s + NS - 1) % NS
    is_share = (bz8 >= 2) & (bz8 < 6)
    my_cell = bx * 4 + bz8 - 2
    even = s % 2 == 0
    near = jnp.where(even, 2, 0)
    far = jnp.where(even, 0, 2)

    barrier = pltpu.get_barrier_semaphore()

    def greet(i, _):
        other = (b + 1 + i) % NB
        pl.semaphore_signal(barrier, inc=1, device_id={"bead": other, "space": s}, device_id_type=MESH)
        return 0

    pl.semaphore_signal(barrier, inc=1, device_id={"bead": b, "space": up}, device_id_type=MESH)
    pl.semaphore_signal(barrier, inc=1, device_id={"bead": b, "space": down}, device_id_type=MESH)
    lax.fori_loop(0, NB - 1, greet, 0)

    def spread(ref_row):
        return jnp.broadcast_to(ref_row, (128, 128)).T

    def prep(c, _):
        for d in range(4):
            xi[d, c] = spread(own_ref[d, pl.ds(c, 1), :])
        for d in range(3):
            acc[d, c] = jnp.zeros((128, 128), F32)
        return 0

    lax.fori_loop(0, 16, prep, 0)

    def short_pairs(src, base_row, y, y2, shift):
        for z in range(4):
            i = y * 4 + z
            cols = []
            for z2 in range(max(z - 1, 0), min(z + 2, 4)):
                row = y2 * 4 + z2
                xj = src(0, row)
                if shift is not None:
                    xj = xj + shift
                cols.append([jnp.broadcast_to(v, (8, 128)) for v in (xj, src(1, row), src(2, row), src(3, row), src(4, row))])
            for t in range(16):
                lanes = pl.ds(8 * t, 8)
                xa, ya, za, sa = (xi[d, i, lanes, :] for d in range(4))
                tot = [acc[d, i, lanes, :] for d in range(3)]
                for xj, yj, zj, sj, ej in cols:
                    dx = xa - xj
                    dy = ya - yj
                    dz = za - zj
                    r2 = dx * dx + dy * dy + dz * dz
                    sp = sa + sj
                    s2 = sp * sp
                    p = 1.0 / (r2 + s2)
                    m = jnp.maximum(1.0 - r2, 0.0)
                    q = s2 * p
                    w = q * q * q
                    pm = p * m
                    bb = pm + (2.0 / 3.0)
                    g = (w * m) * (w * (pm + bb) - bb) * ej
                    tot = [tot[0] + g * dx, tot[1] + g * dy, tot[2] + g * dz]
                for d in range(3):
                    acc[d, i, lanes, :] = tot[d]

    def own_src(d, row):
        return own_ref[d, pl.ds(row, 1), :]

    def own_row(n, _):
        y = n // 3
        y2 = y + n % 3 - 1

        @pl.when((y2 >= 0) & (y2 < 4))
        def _():
            short_pairs(own_src, None, y, y2, None)
        return 0

    lax.fori_loop(0, 7, own_row, 0)

    pl.semaphore_wait(barrier, NB + 1)

    halo_up = pltpu.make_async_remote_copy(
        src_ref=own_ref, dst_ref=ext.at[0], send_sem=halo_ss.at[0], recv_sem=halo_rs.at[0],
        device_id={"bead": b, "space": up}, device_id_type=MESH)
    halo_down = pltpu.make_async_remote_copy(
        src_ref=own_ref, dst_ref=ext.at[1], send_sem=halo_ss.at[1], recv_sem=halo_rs.at[1],
        device_id={"bead": b, "space": down}, device_id_type=MESH)
    halo_up.start()
    halo_down.start()

    def to_share(src, dst, ss, rs, c):
        target = share_bead(c)

        @pl.when(target != b)
        def _():
            pltpu.make_async_remote_copy(
                src_ref=src.at[c], dst_ref=dst.at[b], send_sem=ss.at[c], recv_sem=rs,
                device_id={"bead": target, "space": s}, device_id_type=MESH).start()

        @pl.when(target == b)
        def _():
            pltpu.make_async_copy(src.at[c], dst.at[b], rs).start()

    def sent_share(src, dst, ss, rs, c):
        target = share_bead(c)

        @pl.when(target != b)
        def _():
            pltpu.make_async_remote_copy(
                src_ref=src.at[c], dst_ref=dst.at[b], send_sem=ss.at[c], recv_sem=rs,
                device_id={"bead": target, "space": s}, device_id_type=MESH).wait_send()

    def send_early(c, _):
        to_share(early_ref, eb, early_ss, early_rs, c)
        return 0

    lax.fori_loop(0, 16, send_early, 0)
    lax.fori_loop(7, 12, own_row, 0)

    def ext_src(k):
        return lambda d, row: ext[k, d, pl.ds(row, 1), :]

    def wait_halo(side):
        pltpu.make_async_remote_copy(
            src_ref=own_ref, dst_ref=ext.at[side], send_sem=halo_ss.at[side], recv_sem=halo_rs.at[side],
            device_id={"bead": b, "space": up}, device_id_type=MESH).wait_recv()

    def both(which):
        side = jnp.where(even, 1 - which, which)
        shift = jnp.where(side == 1, 2.0, -2.0)
        return side, shift

    near_side, near_shift = both(0)
    far_side, far_shift = both(1)

    wait_halo(near_side)

    def near_row(n, _):
        y = n // 3
        y2 = y + n % 3 - 1

        @pl.when((y2 >= 0) & (y2 < 4))
        def _():
            short_pairs(ext_src(near_side), None, y, y2, near_shift)
        return 0

    lax.fori_loop(0, 12, near_row, 0)

    def mm(a, v):
        return jnp.dot(a, v, preferred_element_type=F32, precision=lax.Precision.HIGHEST)

    @pl.when(is_share)
    def _():
        pltpu.make_async_copy(eb, eb, early_rs).wait()
        for d in range(3):
            mixed[d] = mm(table_ref[0:72, :], eb[:, d, :]) + mm(table_ref[72:144, :], eb[:, 3 + d, :])

    wait_halo(far_side)

    def far_y(y, _):
        def far_row(n, _):
            y2 = y + n - 1

            @pl.when((y2 >= 0) & (y2 < 4))
            def _():
                short_pairs(ext_src(far_side), None, y, y2, far_shift)
            return 0

        lax.fori_loop(0, 3, far_row, 0)
        for z in range(4):
            c = y * 4 + z
            rows = [jnp.sum(acc[d, c].T, 0, keepdims=True) for d in range(3)]
            late_out[c] = aux_ref[c, 0:3, :] + aux_ref[c, 3:4, :] * jnp.concatenate(rows, 0)
        for z in range(4):
            to_share(late_out, kb, late_ss, late_rs, y * 4 + z)
        return 0

    lax.fori_loop(0, 4, far_y, 0)

    def cont_target(n):
        r = n // 12
        q = n % 12 // 3
        e = n % 3
        by = q // 2
        bz = q % 2
        jy = my_cell // 4 - by
        jz = my_cell % 4 - bz
        ok = is_share & (jy >= 0) & (jy < 3) & (jz >= 0) & (jz < 3)
        tb = (r % 4) * 8 + (r // 4) * 4 + q
        ts = (s + e + NS - 1) % NS
        slot = 2 - e
        return ok, r, tb, ts, slot, jy, jz, e

    def cont_copy(n):
        ok, r, tb, ts, slot, jy, jz, e = cont_target(n)
        remote = pltpu.make_async_remote_copy(
            src_ref=cont.at[r], dst_ref=cb.at[slot, jy, jz], send_sem=cont_ss.at[n], recv_sem=cont_rs.at[slot],
            device_id={"bead": tb, "space": ts}, device_id_type=MESH)
        local = pltpu.make_async_copy(cont.at[r], cb.at[slot, jy, jz], cont_rs.at[slot])
        mine = (tb == b) & (e == 1)
        return ok, mine, remote, local

    @pl.when(is_share)
    def _():
        pltpu.make_async_copy(kb, kb, late_rs).wait()
        for d in range(3):
            cont[:, d, :] = mixed[d, 64:72, :] + mm(table_ref[208:216, :], kb[:, d, :])

        def send_cont(n, _):
            ok, mine, remote, local = cont_copy(n)

            @pl.when(ok & jnp.logical_not(mine))
            def _():
                remote.start()

            @pl.when(ok & mine)
            def _():
                local.start()
            return 0

        lax.fori_loop(0, 96, send_cont, 0)
        for d in range(3):
            full = mixed[d, 0:64, :] + mm(table_ref[144:208, :], kb[:, d, :])
            ret[:, d, :] = full[0:32]
            ret[:, 3 + d, :] = full[32:64]

        def send_ret(k, _):
            @pl.when(k != b)
            def _():
                pltpu.make_async_remote_copy(
                    src_ref=ret.at[k], dst_ref=rb.at[my_cell], send_sem=ret_ss.at[k], recv_sem=ret_rs,
                    device_id={"bead": k, "space": s}, device_id_type=MESH).start()

            @pl.when(k == b)
            def _():
                pltpu.make_async_copy(ret.at[k], rb.at[my_cell], ret_rs).start()
            return 0

        lax.fori_loop(0, NB, send_ret, 0)

    rhi = bz8 // 4
    q = bz8 % 4
    by = q // 2
    bz = q % 2
    flip = lambda bit, v, top: jnp.where(bit == 1, top - v, v)

    def wait_cont(slot):
        pltpu.make_async_copy(cb.at[slot], cb.at[slot], cont_rs.at[slot]).wait()

    wait_cont(1)
    for iy in range(2):
        for iz in range(2):
            wy = by + iy
            wz = bz + iz
            me = cb[1, wy, wz]
            cell = (2 * by + iy) * 4 + 2 * bz + iz
            xs[0, iy, iz] = spread(2.0 * me[0:1])
            xs[1, iy, iz] = spread(2.0 * (me[1:2] + wy.astype(F32)))
            xs[2, iy, iz] = spread(2.0 * (me[2:3] + wz.astype(F32)))
            xs[3, iy, iz] = spread(own_ref[3, pl.ds(cell, 1), :])
            for d in range(3):
                sacc[d, iy, iz] = jnp.zeros((128, 128), F32)

    Y_PAIRS = ((0, 0), (0, 1), (1, 0), (1, 1), (1, 2))

    def slow_pairs(slot, params, shift):
        def one(n, _):
            fy = jnp.where(n < 2, 0, 1)
            jy = flip(by, jnp.where(n < 2, n, n - 2), 2)
            iy = flip(by, fy, 1)
            js = []
            for jz0 in range(3):
                jz = flip(bz, jz0, 2)
                v = cb[slot, jy, jz]
                row = (by + jy) * 4 + bz + jz
                vals = (2.0 * v[0:1] + shift, 2.0 * (v[1:2] + jy.astype(F32)), 2.0 * (v[2:3] + jz.astype(F32)), params(3, row), params(4, row))
                js.append([jnp.broadcast_to(a, (8, 128)) for a in vals])
            for iz0 in range(2):
                iz = flip(bz, iz0, 1)
                for t in range(16):
                    lanes = pl.ds(8 * t, 8)
                    xa, ya, za, sa = (xs[d, iy, iz, lanes, :] for d in range(4))
                    tot = [sacc[d, iy, iz, lanes, :] for d in range(3)]
                    for jz0 in (range(2) if iz0 == 0 else range(3)):
                        xj, yj, zj, sj, ej = js[jz0]
                        dx = xa - xj
                        dy = ya - yj
                        dz = za - zj
                        r2 = dx * dx + dy * dy + dz * dz
                        sp = sa + sj
                        s2 = sp * sp
                        p = 1.0 / (r2 + s2)
                        m2 = jnp.maximum(1.0 - r2, 0.0)
                        m1 = jnp.maximum(1.0 - 0.25 * r2, 0.0)
                        w = s2 * p
                        w = w * w * w
                        ps = p * (m1 * m1 - m2 * m2)
                        bb = ps + (m1 * (1.0 / 6.0) - m2 * (2.0 / 3.0))
                        g = w * (w * (ps + bb) - bb) * ej
                        tot = [tot[0] + g * dx, tot[1] + g * dy, tot[2] + g * dz]
                    for d in range(3):
                        sacc[d, iy, iz, lanes, :] = tot[d]
            return 0

        lax.fori_loop(0, 5, one, 0)

    slow_pairs(1, own_src, 0.0)
    near_slot = near_side * 2
    far_slot = far_side * 2
    wait_cont(near_slot)
    slow_pairs(near_slot, ext_src(near_side), near_shift)
    wait_cont(far_slot)
    slow_pairs(far_slot, ext_src(far_side), far_shift)

    for iy in range(2):
        for iz in range(2):
            cell = (2 * by + iy) * 4 + 2 * bz + iz
            rows = [jnp.sum(sacc[d, iy, iz].T, 0, keepdims=True) for d in range(3)]
            fb[2 * iy + iz] = aux_ref[cell, 4:5, :] * jnp.concatenate(rows, 0)

    def x_copy(i):
        other = (bx + 1 + i) % 4
        return pltpu.make_async_remote_copy(
            src_ref=fb, dst_ref=xb.at[bx], send_sem=xb_ss.at[i], recv_sem=xb_rs,
            device_id={"bead": other * 8 + bz8, "space": s}, device_id_type=MESH)

    for i in range(3):
        x_copy(i).start()
    pltpu.make_async_copy(fb, xb.at[bx], xb_rs).start()
    pltpu.make_async_copy(xb, xb, xb_rs).wait()

    def z_copy(i):
        other = (bz8 + i) % 8
        return pltpu.make_async_remote_copy(
            src_ref=zs.at[i], dst_ref=zb.at[bz8], send_sem=zb_ss.at[i], recv_sem=zb_rs,
            device_id={"bead": bx * 8 + other, "space": s}, device_id_type=MESH)

    for i in range(8):
        k = bx * 8 + (bz8 + i) % 8
        part = w_ref[rhi * 4, k] * xb[0]
        for x2 in range(1, 4):
            part = part + w_ref[rhi * 4 + x2, k] * xb[x2]
        zs[i] = part
    for i in range(1, 8):
        z_copy(i).start()
    pltpu.make_async_copy(zs.at[0], zb.at[bz8], zb_rs).start()

    pltpu.make_async_copy(rb, rb, ret_rs).wait()
    for c in range(16):
        nx_ref[c] = rb[c, 0:3, :]
    pltpu.make_async_copy(zb, zb, zb_rs).wait()
    for c in range(16):
        y, z = c // 4, c % 4
        blk = (y // 2) * 2 + z // 2
        at = (y % 2) * 2 + z % 2
        np_ref[c] = rb[c, 3:6, :] * aux_ref[c, 5:6, :] + (zb[blk, at] + zb[4 + blk, at])

    halo_up.wait_send()
    halo_down.wait_send()

    def drain(c, _):
        sent_share(early_ref, eb, early_ss, early_rs, c)
        sent_share(late_out, kb, late_ss, late_rs, c)
        return 0

    lax.fori_loop(0, 16, drain, 0)

    @pl.when(is_share)
    def _():
        def drain_cont(n, _):
            ok, mine, remote, local = cont_copy(n)

            @pl.when(ok & jnp.logical_not(mine))
            def _():
                remote.wait_send()
            return 0

        lax.fori_loop(0, 96, drain_cont, 0)

        def drain_ret(k, _):
            @pl.when(k != b)
            def _():
                pltpu.make_async_remote_copy(
                    src_ref=ret.at[k], dst_ref=rb.at[my_cell], send_sem=ret_ss.at[k], recv_sem=ret_rs,
                    device_id={"bead": k, "space": s}, device_id_type=MESH).wait_send()
            return 0

        lax.fori_loop(0, NB, drain_ret, 0)

    for i in range(3):
        x_copy(i).wait_send()
    for i in range(1, 8):
        z_copy(i).wait_send()


def shards(positions, momenta, noise, atom_types, occupancy, type_sigma, type_eps, type_mass):
    table, weights = bead_tables()
    hot = atom_types[..., None] == jnp.arange(4)
    pick = lambda v: jnp.sum(jnp.where(hot, v, 0.0), -1)
    sigma = pick(type_sigma)
    mass = pick(type_mass)
    live = (jnp.arange(128)[None, :] < occupancy[:, None]).astype(F32)
    e = jnp.sqrt(pick(type_eps)) * live
    l = np.arange(16)
    corner = np.stack([np.full(16, -0.5), l // 4 - 2.0, l % 4 - 2.0], 0).astype(np.float32)
    x = positions[0]
    scaled = 2.0 * (jnp.transpose(x, (1, 0, 2)) + corner[:, :, None])
    own = jnp.concatenate([scaled, sigma[None], e[None]], 0)
    early = jnp.concatenate([x, noise[0] / jnp.sqrt(mass)[:, None, :]], 1)
    zero = jnp.zeros_like(e)
    coeff = (0.5 * TIME_STEP * 48.0) * e / mass
    aux = jnp.concatenate(
        [momenta[0] / mass[:, None, :], jnp.stack([coeff, 48.0 * e, mass, zero, zero], 1)], 1)
    vm = pl.BlockSpec(memory_space=pltpu.VMEM)
    out = jax.ShapeDtypeStruct((16, 3, 128), F32)
    V = lambda *shape: pltpu.VMEM(shape, F32)
    D = pltpu.SemaphoreType.DMA
    nx, pn = pl.pallas_call(
        kernel,
        out_shape=(out, out),
        in_specs=[vm, vm, vm, vm, pl.BlockSpec(memory_space=pltpu.SMEM)],
        out_specs=(vm, vm),
        scratch_shapes=[
            V(2, 5, 16, 128), V(4, 16, 128, 128), V(3, 16, 128, 128), V(32, 6, 128), V(32, 3, 128),
            V(16, 3, 128), V(3, 72, 128), V(8, 3, 128), V(32, 6, 128), V(16, 6, 128), V(3, 3, 3, 3, 128),
            V(4, 2, 2, 128, 128), V(3, 2, 2, 128, 128), V(4, 3, 128), V(4, 4, 3, 128), V(8, 4, 3, 128), V(8, 4, 3, 128),
            D((2,)), D((2,)), D((16,)), D, D((16,)), D, D((96,)), D((3,)), D((32,)), D, D((3,)), D, D((8,)), D,
        ],
        compiler_params=pltpu.CompilerParams(collective_id=0, has_side_effects=True, vmem_limit_bytes=40 << 20),
    )(own, early, aux, jnp.asarray(table), jnp.asarray(weights))
    return nx[None], pn[None]


def solution(mesh):
    full = P("bead", "space", None, None)
    placed = (full, full, full, P("space", None), P("space"), P(), P(), P())
    return jax.shard_map(shards, mesh=mesh, in_specs=placed, out_specs=(full, full), check_vma=False)
```

```python
import functools
import math

import jax
import jax.numpy as jnp
import numpy as np
from jax import lax
from jax.experimental import pallas as pl
from jax.experimental.pallas import tpu as pltpu
from jax.sharding import PartitionSpec as P

F32 = jnp.float32
MESH = pl.DeviceIdType.MESH
NB = 32
NS = 16
PC = 8
TIME_STEP = 0.05
INVERSE_TEMP = 32.0
CENTROID_FRICTION = 1.0


def mode_table(n):
    k = np.arange(n)[:, None].astype(np.float64)
    m = np.arange(n)[None, :].astype(np.float64)
    phase = 2.0 * np.pi * k * m / n
    c = np.where(m < n / 2, np.sqrt(2.0 / n) * np.cos(phase), np.sqrt(2.0 / n) * np.sin(phase))
    c = np.where(m == n / 2, np.cos(np.pi * k) / np.sqrt(n), c)
    return np.where(m == 0, 1.0 / np.sqrt(n), c)


def bead_tables():
    c = mode_table(NB)
    n = np.arange(NB)
    freq = 2.0 * (NB / INVERSE_TEMP) * np.sin(np.pi * n / NB)
    gamma = np.where(n == 0, CENTROID_FRICTION, 2.0 * freq)
    c1 = np.exp(-gamma * TIME_STEP)
    kick = np.sqrt((1.0 - c1 * c1) / INVERSE_TEMP)
    cosine = np.cos(freq * TIME_STEP)
    sine = np.sin(freq * TIME_STEP)
    drift = np.where(n == 0, TIME_STEP, sine / np.where(n == 0, 1.0, freq))

    def mix(d):
        return (c * d[None, :]) @ c.T

    pick = np.arange(PC)
    pick = np.where(pick <= PC // 2, pick, pick + NB - PC)
    w = np.sqrt(PC / NB) * mode_table(PC) @ c[:, pick].T
    x_from = (mix(cosine), mix(drift * kick), mix(drift * c1))
    p_from = (mix(-freq * sine), mix(cosine * kick), mix(cosine * c1))
    early_x = np.concatenate([x_from[0], p_from[0], w @ x_from[0]], 0)
    early_n = np.concatenate([x_from[1], p_from[1], w @ x_from[1]], 0)
    late = np.concatenate([x_from[2], p_from[2], w @ x_from[2]], 0)
    table = np.concatenate([early_x, early_n, late], 0).astype(np.float32)
    weights = (w * (0.5 * TIME_STEP * NB / PC)).astype(np.float32)
    return table, weights


def share_bead(cell):
    return (cell // 4) * 8 + 2 + cell % 4


def kernel(pos_in, mom_in, noise_in, types_in, occ_in, sig_in, eps_in, mass_in, table_in, w_in, nx_ref, np_ref,
           pos, mom, noise, types, table_ref, occ, ts_sig, ts_eps, ts_mass, w_ref,
           own_ref, early_ref, pm, invm, kcoef, e48, mass, slots,
           ext, xi, acc, eb, kb, late_out, mixed, cont, ret, rb, cb, xs, sacc, fb, xb, zs, zb,
           in_s, halo_ss, halo_rs, early_ss, early_rs, late_ss, late_rs, cont_ss, cont_own_ss, cont_rs, ret_ss, ret_rs,
           xb_ss, xb_rs, zb_ss, zb_rs):
    b = lax.axis_index("bead")
    s = lax.axis_index("space")
    bx = b // 8
    bz8 = b % 8
    up = (s + 1) % NS
    down = (s + NS - 1) % NS
    is_share = (bz8 >= 2) & (bz8 < 6)
    my_cell = bx * 4 + bz8 - 2
    even = s % 2 == 0

    barrier = pltpu.get_barrier_semaphore()

    def greet(i, _):
        other = (b + 1 + i) % NB
        pl.semaphore_signal(barrier, inc=1, device_id={"bead": other, "space": s}, device_id_type=MESH)
        return 0

    pl.semaphore_signal(barrier, inc=1, device_id={"bead": b, "space": up}, device_id_type=MESH)
    pl.semaphore_signal(barrier, inc=1, device_id={"bead": b, "space": down}, device_id_type=MESH)
    lax.fori_loop(0, NB - 1, greet, 0)

    loads = [
        pltpu.make_async_copy(src, dst, in_s.at[i])
        for i, (src, dst) in enumerate((
            (occ_in, occ), (sig_in, ts_sig), (eps_in, ts_eps), (mass_in, ts_mass), (types_in, types),
            (pos_in, pos), (mom_in, mom), (noise_in, noise), (table_in, table_ref), (w_in, w_ref)))
    ]
    for load in loads:
        load.start()
    for load in loads:
        load.wait()

    kind = types[...]

    def pick(tab):
        v = jnp.where(kind == 0, tab[0], tab[1])
        v = jnp.where(kind == 2, tab[2], v)
        return jnp.where(kind == 3, tab[3], v)

    m_all = pick(ts_mass)
    inv = 1.0 / m_all
    slot_index = lax.broadcasted_iota(jnp.int32, (1, 128), 1)
    live = jnp.concatenate([jnp.where(slot_index < occ[c], 1.0, 0.0) for c in range(16)], 0)
    e_all = jnp.sqrt(pick(ts_eps)) * live
    mass[...] = m_all
    invm[...] = inv
    e48[...] = 48.0 * e_all
    kcoef[...] = (0.5 * TIME_STEP * 48.0) * e_all * inv
    root = jnp.sqrt(inv)
    cell_of = lax.broadcasted_iota(jnp.int32, (16, 128), 0)
    corner = (-0.5, (cell_of // 4).astype(F32) - 2.0, (cell_of % 4).astype(F32) - 2.0)
    for d in range(3):
        own_ref[d] = 2.0 * (pos[0, d] + corner[d])
        early_ref[:, d, :] = pos[0, d]
        early_ref[:, 3 + d, :] = noise[0, d] * root
        pm[:, d, :] = mom[0, d] * inv
    own_ref[3] = pick(ts_sig)
    own_ref[4] = e_all

    def spread(ref_row):
        return jnp.broadcast_to(ref_row, (128, 128)).T

    def prep(c, _):
        for d in range(4):
            xi[d, c] = spread(own_ref[d, pl.ds(c, 1), :])
        for d in range(3):
            acc[d, c] = jnp.zeros((128, 128), F32)
        return 0

    lax.fori_loop(0, 16, prep, 0)

    def short_pairs(src, base_row, y, y2, shift):
        for z in range(4):
            i = y * 4 + z
            cols = []
            for z2 in range(max(z - 1, 0), min(z + 2, 4)):
                row = y2 * 4 + z2
                xj = src(0, row)
                if shift is not None:
                    xj = xj + shift
                cols.append([jnp.broadcast_to(v, (8, 128)) for v in (xj, src(1, row), src(2, row), src(3, row), src(4, row))])
            for t in range(16):
                lanes = pl.ds(8 * t, 8)
                xa, ya, za, sa = (xi[d, i, lanes, :] for d in range(4))
                tot = [acc[d, i, lanes, :] for d in range(3)]
                for xj, yj, zj, sj, ej in cols:
                    dx = xa - xj
                    dy = ya - yj
                    dz = za - zj
                    r2 = dx * dx + dy * dy + dz * dz
                    sp = sa + sj
                    s2 = sp * sp
                    p = 1.0 / (r2 + s2)
                    m = jnp.maximum(1.0 - r2, 0.0)
                    q = s2 * p
                    w = q * q * q
                    pm = p * m
                    bb = pm + (2.0 / 3.0)
                    g = (w * m) * (w * (pm + bb) - bb) * ej
                    tot = [tot[0] + g * dx, tot[1] + g * dy, tot[2] + g * dz]
                for d in range(3):
                    acc[d, i, lanes, :] = tot[d]

    def own_src(d, row):
        return own_ref[d, pl.ds(row, 1), :]

    def own_row(n, _):
        y = n // 3
        y2 = y + n % 3 - 1

        @pl.when((y2 >= 0) & (y2 < 4))
        def _():
            short_pairs(own_src, None, y, y2, None)
        return 0

    lax.fori_loop(0, 7, own_row, 0)

    pl.semaphore_wait(barrier, NB + 1)

    halo_up = pltpu.make_async_remote_copy(
        src_ref=own_ref, dst_ref=ext.at[0], send_sem=halo_ss.at[0], recv_sem=halo_rs.at[0],
        device_id={"bead": b, "space": up}, device_id_type=MESH)
    halo_down = pltpu.make_async_remote_copy(
        src_ref=own_ref, dst_ref=ext.at[1], send_sem=halo_ss.at[1], recv_sem=halo_rs.at[1],
        device_id={"bead": b, "space": down}, device_id_type=MESH)
    halo_up.start()
    halo_down.start()

    def to_share(src, dst, ss, rs, c):
        target = share_bead(c)

        @pl.when(target != b)
        def _():
            pltpu.make_async_remote_copy(
                src_ref=src.at[c], dst_ref=dst.at[b], send_sem=ss, recv_sem=rs,
                device_id={"bead": target, "space": s}, device_id_type=MESH).start()

        @pl.when(target == b)
        def _():
            pltpu.make_async_copy(src.at[c], dst.at[b], rs).start()

    def sent_share(src, ss):
        @pl.when(is_share)
        def _():
            pltpu.make_async_copy(src.at[pl.ds(0, 15)], src.at[pl.ds(0, 15)], ss).wait()

        @pl.when(jnp.logical_not(is_share))
        def _():
            pltpu.make_async_copy(src, src, ss).wait()

    def send_early(c, _):
        to_share(early_ref, eb, early_ss, early_rs, c)
        return 0

    lax.fori_loop(0, 16, send_early, 0)
    lax.fori_loop(7, 12, own_row, 0)

    def ext_src(k):
        return lambda d, row: ext[k, d, pl.ds(row, 1), :]

    def wait_halo(side):
        pltpu.make_async_remote_copy(
            src_ref=own_ref, dst_ref=ext.at[side], send_sem=halo_ss.at[side], recv_sem=halo_rs.at[side],
            device_id={"bead": b, "space": up}, device_id_type=MESH).wait_recv()

    def both(which):
        side = jnp.where(even, 1 - which, which)
        shift = jnp.where(side == 1, 2.0, -2.0)
        return side, shift

    near_side, near_shift = both(0)
    far_side, far_shift = both(1)

    wait_halo(near_side)

    def near_row(n, _):
        y = n // 3
        y2 = y + n % 3 - 1

        @pl.when((y2 >= 0) & (y2 < 4))
        def _():
            short_pairs(ext_src(near_side), None, y, y2, near_shift)
        return 0

    lax.fori_loop(0, 12, near_row, 0)

    def mm(a, v):
        return jnp.dot(a, v, preferred_element_type=F32, precision=lax.Precision.HIGHEST)

    @pl.when(is_share)
    def _():
        pltpu.make_async_copy(eb, eb, early_rs).wait()
        for d in range(3):
            mixed[d] = mm(table_ref[0:72, :], eb[:, d, :]) + mm(table_ref[72:144, :], eb[:, 3 + d, :])

    halo_up.wait_send()
    halo_down.wait_send()
    sent_share(early_ref, early_ss)
    wait_halo(far_side)

    def far_y(y, _):
        def far_row(n, _):
            y2 = y + n - 1

            @pl.when((y2 >= 0) & (y2 < 4))
            def _():
                short_pairs(ext_src(far_side), None, y, y2, far_shift)
            return 0

        lax.fori_loop(0, 3, far_row, 0)
        for z in range(4):
            c = y * 4 + z
            rows = [jnp.sum(acc[d, c].T, 0, keepdims=True) for d in range(3)]
            late_out[c] = pm[c] + kcoef[pl.ds(c, 1), :] * jnp.concatenate(rows, 0)
        for z in range(4):
            to_share(late_out, kb, late_ss, late_rs, y * 4 + z)
        return 0

    lax.fori_loop(0, 4, far_y, 0)

    my_y = my_cell // 4
    my_z = my_cell % 4
    y_first, y_last = jnp.where(my_y == 3, 1, 0), jnp.where(my_y == 0, 1, 2)
    z_first, z_last = jnp.where(my_z == 3, 1, 0), jnp.where(my_z == 0, 1, 2)
    blocks = (y_last - y_first) * (z_last - z_first)
    far_space = jnp.where(even, down, up)
    near_space = jnp.where(even, up, down)
    far_dst = jnp.where(even, 2, 0)
    near_dst = jnp.where(even, 0, 2)
    my_r = (bz8 // 4) * 4 + bx
    has_own = is_share & (my_y - (bz8 % 4) // 2 >= 0) & (my_y - (bz8 % 4) // 2 < 3) & (
        my_z - bz8 % 2 >= 0) & (my_z - bz8 % 2 < 3)

    def over_blocks(body):
        def outer(by, _):
            def inner(bz, _):
                body(by * 2 + bz, my_y - by, my_z - bz)
                return 0

            return lax.fori_loop(z_first, z_last, inner, 0)

        lax.fori_loop(y_first, y_last, outer, 0)

    @pl.when(is_share)
    def _():
        pltpu.make_async_copy(kb, kb, late_rs).wait()
        for d in range(3):
            cont[:, d, :] = mixed[d, 64:72, :] + mm(table_ref[208:216, :], kb[:, d, :])

        def outside(space, slot):
            def body(q, jy, jz):
                for r in range(PC):
                    pltpu.make_async_remote_copy(
                        src_ref=cont.at[r], dst_ref=cb.at[slot, jy, jz], send_sem=cont_ss, recv_sem=cont_rs.at[slot],
                        device_id={"bead": (r % 4) * 8 + (r // 4) * 4 + q, "space": space}, device_id_type=MESH).start()
            over_blocks(body)

        outside(far_space, far_dst)
        outside(near_space, near_dst)

        def inside(q, jy, jz):
            for r in range(PC):
                tb = (r % 4) * 8 + (r // 4) * 4 + q

                @pl.when(tb != b)
                def _():
                    pltpu.make_async_remote_copy(
                        src_ref=cont.at[r], dst_ref=cb.at[1, jy, jz], send_sem=cont_own_ss, recv_sem=cont_rs.at[1],
                        device_id={"bead": tb, "space": s}, device_id_type=MESH).start()

                @pl.when(tb == b)
                def _():
                    pltpu.make_async_copy(cont.at[r], cb.at[1, jy, jz], cont_rs.at[1]).start()

        over_blocks(inside)
        for d in range(3):
            full = mixed[d, 0:64, :] + mm(table_ref[144:208, :], kb[:, d, :])
            ret[:, d, :] = full[0:32]
            ret[:, 3 + d, :] = full[32:64]

        def send_ret(k, _):
            @pl.when(k != b)
            def _():
                pltpu.make_async_remote_copy(
                    src_ref=ret.at[k], dst_ref=rb.at[my_cell], send_sem=ret_ss, recv_sem=ret_rs,
                    device_id={"bead": k, "space": s}, device_id_type=MESH).start()

            @pl.when(k == b)
            def _():
                pltpu.make_async_copy(ret.at[k], rb.at[my_cell], ret_rs).start()
            return 0

        lax.fori_loop(0, NB, send_ret, 0)

    rhi = bz8 // 4
    q = bz8 % 4
    by = q // 2
    bz = q % 2
    flip = lambda bit, v, top: jnp.where(bit == 1, top - v, v)

    def wait_cont(slot):
        pltpu.make_async_copy(cb.at[slot], cb.at[slot], cont_rs.at[slot]).wait()

    wait_cont(1)
    for iy in range(2):
        for iz in range(2):
            wy = by + iy
            wz = bz + iz
            me = cb[1, wy, wz]
            cell = (2 * by + iy) * 4 + 2 * bz + iz
            xs[0, iy, iz] = spread(2.0 * me[0:1])
            xs[1, iy, iz] = spread(2.0 * (me[1:2] + wy.astype(F32)))
            xs[2, iy, iz] = spread(2.0 * (me[2:3] + wz.astype(F32)))
            xs[3, iy, iz] = spread(own_ref[3, pl.ds(cell, 1), :])
            for d in range(3):
                sacc[d, iy, iz] = jnp.zeros((128, 128), F32)

    Y_PAIRS = ((0, 0), (0, 1), (1, 0), (1, 1), (1, 2))

    def slow_pairs(slot, params, shift):
        def one(n, _):
            fy = jnp.where(n < 2, 0, 1)
            jy = flip(by, jnp.where(n < 2, n, n - 2), 2)
            iy = flip(by, fy, 1)
            js = []
            for jz0 in range(3):
                jz = flip(bz, jz0, 2)
                v = cb[slot, jy, jz]
                row = (by + jy) * 4 + bz + jz
                vals = (2.0 * v[0:1] + shift, 2.0 * (v[1:2] + jy.astype(F32)), 2.0 * (v[2:3] + jz.astype(F32)), params(3, row), params(4, row))
                js.append([jnp.broadcast_to(a, (8, 128)) for a in vals])
            for iz0 in range(2):
                iz = flip(bz, iz0, 1)
                for t in range(16):
                    lanes = pl.ds(8 * t, 8)
                    xa, ya, za, sa = (xs[d, iy, iz, lanes, :] for d in range(4))
                    tot = [sacc[d, iy, iz, lanes, :] for d in range(3)]
                    for jz0 in (range(2) if iz0 == 0 else range(3)):
                        xj, yj, zj, sj, ej = js[jz0]
                        dx = xa - xj
                        dy = ya - yj
                        dz = za - zj
                        r2 = dx * dx + dy * dy + dz * dz
                        sp = sa + sj
                        s2 = sp * sp
                        p = 1.0 / (r2 + s2)
                        m2 = jnp.maximum(1.0 - r2, 0.0)
                        m1 = jnp.maximum(1.0 - 0.25 * r2, 0.0)
                        w = s2 * p
                        w = w * w * w
                        ps = p * (m1 * m1 - m2 * m2)
                        bb = ps + (m1 * (1.0 / 6.0) - m2 * (2.0 / 3.0))
                        g = w * (w * (ps + bb) - bb) * ej
                        tot = [tot[0] + g * dx, tot[1] + g * dy, tot[2] + g * dz]
                    for d in range(3):
                        sacc[d, iy, iz, lanes, :] = tot[d]
            return 0

        lax.fori_loop(0, 5, one, 0)

    slow_pairs(1, own_src, 0.0)
    near_slot = near_side * 2
    far_slot = far_side * 2
    wait_cont(near_slot)
    slow_pairs(near_slot, ext_src(near_side), near_shift)
    wait_cont(far_slot)
    slow_pairs(far_slot, ext_src(far_side), far_shift)

    for iy in range(2):
        for iz in range(2):
            cell = (2 * by + iy) * 4 + 2 * bz + iz
            rows = [jnp.sum(sacc[d, iy, iz].T, 0, keepdims=True) for d in range(3)]
            fb[2 * iy + iz] = e48[pl.ds(cell, 1), :] * jnp.concatenate(rows, 0)

    def x_copy(i):
        other = (bx + 1 + i) % 4
        return pltpu.make_async_remote_copy(
            src_ref=fb, dst_ref=xb.at[bx], send_sem=xb_ss.at[i], recv_sem=xb_rs,
            device_id={"bead": other * 8 + bz8, "space": s}, device_id_type=MESH)

    for i in range(3):
        x_copy(i).start()
    pltpu.make_async_copy(fb, xb.at[bx], xb_rs).start()
    pltpu.make_async_copy(rb, rb, ret_rs).wait()
    for d in range(3):
        nx_ref[0, d] = rb[:, d, :]
        np_ref[0, d] = rb[:, 3 + d, :] * mass[...]
    sent_share(late_out, late_ss)

    def wait_slots(sem, n):
        pltpu.make_async_copy(slots.at[pl.ds(0, n)], slots.at[pl.ds(0, n)], sem).wait()

    for nq in (1, 2, 4):
        @pl.when(is_share & (blocks == nq))
        def _():
            wait_slots(cont_ss, 16 * nq)

        @pl.when(is_share & (blocks == nq) & has_own)
        def _():
            wait_slots(cont_own_ss, 8 * nq - 1)

        @pl.when(is_share & (blocks == nq) & jnp.logical_not(has_own))
        def _():
            wait_slots(cont_own_ss, 8 * nq)

    @pl.when(is_share)
    def _():
        pltpu.make_async_copy(ret.at[pl.ds(0, NB - 1)], ret.at[pl.ds(0, NB - 1)], ret_ss).wait()

    pltpu.make_async_copy(xb, xb, xb_rs).wait()

    def z_copy(i):
        other = (bz8 + i) % 8
        return pltpu.make_async_remote_copy(
            src_ref=zs.at[i], dst_ref=zb.at[bz8], send_sem=zb_ss.at[i], recv_sem=zb_rs,
            device_id={"bead": bx * 8 + other, "space": s}, device_id_type=MESH)

    for i in range(8):
        k = bx * 8 + (bz8 + i) % 8
        part = w_ref[rhi * 4, k] * xb[0]
        for x2 in range(1, 4):
            part = part + w_ref[rhi * 4 + x2, k] * xb[x2]
        zs[i] = part
    for i in range(1, 8):
        z_copy(i).start()
    pltpu.make_async_copy(zs.at[0], zb.at[bz8], zb_rs).start()

    pltpu.make_async_copy(zb, zb, zb_rs).wait()
    slow = []
    for c in range(16):
        blk = (c // 8) * 2 + (c % 4) // 2
        at = (c // 4 % 2) * 2 + c % 2
        slow.append(zb[blk, at] + zb[4 + blk, at])
    for d in range(3):
        np_ref[0, d] = np_ref[0, d] + jnp.concatenate([v[d:d + 1] for v in slow], 0)
    for i in range(3):
        x_copy(i).wait_send()
    for i in range(1, 8):
        z_copy(i).wait_send()


def shards(positions, momenta, noise, atom_types, occupancy, type_sigma, type_eps, type_mass):
    table, weights = bead_tables()
    anywhere = pl.BlockSpec(memory_space=pltpu.HBM)
    vm = pl.BlockSpec(memory_space=pltpu.VMEM)
    out = jax.ShapeDtypeStruct((1, 3, 16, 128), F32)
    V = lambda *shape: pltpu.VMEM(shape, F32)
    S = lambda shape, kind: pltpu.SMEM(shape, kind)
    D = pltpu.SemaphoreType.DMA
    flip = lambda v: jnp.transpose(v, (0, 2, 1, 3))
    nx, pn = pl.pallas_call(
        kernel,
        out_shape=(out, out),
        in_specs=[anywhere] * 10,
        out_specs=(vm, vm),
        scratch_shapes=[
            V(1, 3, 16, 128), V(1, 3, 16, 128), V(1, 3, 16, 128), pltpu.VMEM((16, 128), jnp.int32), V(216, 32),
            S((16,), jnp.int32), S((4,), F32), S((4,), F32), S((4,), F32), S((PC, NB), F32),
            V(5, 16, 128), V(16, 6, 128), V(16, 3, 128), V(16, 128), V(16, 128), V(16, 128), V(16, 128), V(64, 3, 128),
            V(2, 5, 16, 128), V(4, 16, 128, 128), V(3, 16, 128, 128), V(32, 6, 128), V(32, 3, 128),
            V(16, 3, 128), V(3, 72, 128), V(8, 3, 128), V(32, 6, 128), V(16, 6, 128), V(3, 3, 3, 3, 128),
            V(4, 2, 2, 128, 128), V(3, 2, 2, 128, 128), V(4, 3, 128), V(4, 4, 3, 128), V(8, 4, 3, 128), V(8, 4, 3, 128),
            D((10,)), D((2,)), D((2,)), D, D, D, D, D, D, D((3,)), D, D, D((3,)), D, D((8,)), D,
        ],
        compiler_params=pltpu.CompilerParams(collective_id=0, has_side_effects=True, vmem_limit_bytes=67043328),
    )(flip(positions), flip(momenta), flip(noise), atom_types, occupancy, type_sigma, type_eps, type_mass,
      jnp.asarray(table), jnp.asarray(weights))
    return flip(nx), flip(pn)


def solution(mesh):
    full = P("bead", "space", None, None)
    placed = (full, full, full, P("space", None), P("space"), P(), P(), P())
    return jax.shard_map(shards, mesh=mesh, in_specs=placed, out_specs=(full, full), check_vma=False)
```

```python
import functools
import math

import jax
import jax.numpy as jnp
import numpy as np
from jax import lax
from jax.experimental import pallas as pl
from jax.experimental.pallas import tpu as pltpu
from jax.sharding import PartitionSpec as P

F32 = jnp.float32
MESH = pl.DeviceIdType.MESH
NB = 32
NS = 16
PC = 8
TIME_STEP = 0.05
INVERSE_TEMP = 32.0
CENTROID_FRICTION = 1.0


def mode_table(n):
    k = np.arange(n)[:, None].astype(np.float64)
    m = np.arange(n)[None, :].astype(np.float64)
    phase = 2.0 * np.pi * k * m / n
    c = np.where(m < n / 2, np.sqrt(2.0 / n) * np.cos(phase), np.sqrt(2.0 / n) * np.sin(phase))
    c = np.where(m == n / 2, np.cos(np.pi * k) / np.sqrt(n), c)
    return np.where(m == 0, 1.0 / np.sqrt(n), c)


def bead_tables():
    c = mode_table(NB)
    n = np.arange(NB)
    freq = 2.0 * (NB / INVERSE_TEMP) * np.sin(np.pi * n / NB)
    gamma = np.where(n == 0, CENTROID_FRICTION, 2.0 * freq)
    c1 = np.exp(-gamma * TIME_STEP)
    kick = np.sqrt((1.0 - c1 * c1) / INVERSE_TEMP)
    cosine = np.cos(freq * TIME_STEP)
    sine = np.sin(freq * TIME_STEP)
    drift = np.where(n == 0, TIME_STEP, sine / np.where(n == 0, 1.0, freq))

    def mix(d):
        return (c * d[None, :]) @ c.T

    pick = np.arange(PC)
    pick = np.where(pick <= PC // 2, pick, pick + NB - PC)
    w = np.sqrt(PC / NB) * mode_table(PC) @ c[:, pick].T
    x_from = (mix(cosine), mix(drift * kick), mix(drift * c1))
    p_from = (mix(-freq * sine), mix(cosine * kick), mix(cosine * c1))
    early_x = np.concatenate([x_from[0], p_from[0], w @ x_from[0]], 0)
    early_n = np.concatenate([x_from[1], p_from[1], w @ x_from[1]], 0)
    late = np.concatenate([x_from[2], p_from[2], w @ x_from[2]], 0)
    table = np.concatenate([early_x, early_n, late], 0).astype(np.float32)
    weights = (w * (0.5 * TIME_STEP * NB / PC)).astype(np.float32)
    return table, weights


def share_bead(cell):
    return (cell // 4) * 8 + 2 + cell % 4


def kernel(pos_in, mom_in, noise_in, types_in, occ_in, sig_in, eps_in, mass_in, table_in, w_in, nx_ref, np_ref,
           pos, mom, noise, types, table_ref, occ, ts_sig, ts_eps, ts_mass, w_ref,
           own_ref, early_ref, pm, kcoef, e48, mass, slots, acc_own, acc_j, acc_n, base, react_out, react_in,
           ext, xi, acc, eb, kb, late_out, mixed, cont, ret, rb, cb, xs, sacc, fb, xb, zs, zb,
           in_s, halo_ss, halo_rs, early_ss, early_rs, late_ss, late_rs, cont_ss, cont_own_ss, cont_rs, ret_ss, ret_rs,
           xb_ss, xb_rs, zb_ss, zb_rs, react_ss, react_rs):
    b = lax.axis_index("bead")
    s = lax.axis_index("space")
    bx = b // 8
    bz8 = b % 8
    up = (s + 1) % NS
    down = (s + NS - 1) % NS
    is_share = (bz8 >= 2) & (bz8 < 6)
    my_cell = bx * 4 + bz8 - 2
    even = s % 2 == 0

    barrier = pltpu.get_barrier_semaphore()

    def greet(i, _):
        other = (b + 1 + i) % NB
        pl.semaphore_signal(barrier, inc=1, device_id={"bead": other, "space": s}, device_id_type=MESH)
        return 0

    pl.semaphore_signal(barrier, inc=1, device_id={"bead": b, "space": up}, device_id_type=MESH)
    pl.semaphore_signal(barrier, inc=1, device_id={"bead": b, "space": down}, device_id_type=MESH)
    lax.fori_loop(0, NB - 1, greet, 0)

    loads = [
        pltpu.make_async_copy(src, dst, in_s.at[i])
        for i, (src, dst) in enumerate((
            (occ_in, occ), (sig_in, ts_sig), (eps_in, ts_eps), (mass_in, ts_mass), (types_in, types),
            (pos_in, pos), (mom_in, mom), (noise_in, noise), (table_in, table_ref), (w_in, w_ref)))
    ]
    for load in loads:
        load.start()
    for load in loads:
        load.wait()

    kind = types[...]

    def pick(tab):
        v = jnp.where(kind == 0, tab[0], tab[1])
        v = jnp.where(kind == 2, tab[2], v)
        return jnp.where(kind == 3, tab[3], v)

    m_all = pick(ts_mass)
    inv = 1.0 / m_all
    slot_index = lax.broadcasted_iota(jnp.int32, (1, 128), 1)
    live = jnp.concatenate([jnp.where(slot_index < occ[c], 1.0, 0.0) for c in range(16)], 0)
    e_all = jnp.sqrt(pick(ts_eps)) * live
    mass[...] = m_all
    e48[...] = 48.0 * e_all
    kcoef[...] = (0.5 * TIME_STEP * 48.0) * inv
    for d in range(3):
        acc_j[d] = jnp.zeros((16, 8, 128), F32)
        acc_n[d] = jnp.zeros((16, 8, 128), F32)
    root = jnp.sqrt(inv)
    cell_of = lax.broadcasted_iota(jnp.int32, (16, 128), 0)
    corner = (-0.5, (cell_of // 4).astype(F32) - 2.0, (cell_of % 4).astype(F32) - 2.0)
    for d in range(3):
        own_ref[d] = 2.0 * (pos[0, d] + corner[d])
        early_ref[:, d, :] = pos[0, d]
        early_ref[:, 3 + d, :] = noise[0, d] * root
        pm[:, d, :] = mom[0, d] * inv
    own_ref[3] = pick(ts_sig)
    own_ref[4] = e_all

    def spread(ref_row):
        return jnp.broadcast_to(ref_row, (128, 128)).T

    def prep(c, _):
        for d in range(5):
            xi[d, c] = spread(own_ref[d, pl.ds(c, 1), :])
        return 0

    lax.fori_loop(0, 16, prep, 0)

    def right_data(src, row, shift):
        xj = src(0, row)
        if shift is not None:
            xj = xj + shift
        return [jnp.broadcast_to(v, (8, 128)) for v in (xj, src(1, row), src(2, row), src(3, row), src(4, row))]

    def short_weight(left, right):
        dx = left[0] - right[0]
        dy = left[1] - right[1]
        dz = left[2] - right[2]
        r2 = dx * dx + dy * dy + dz * dz
        sp = left[3] + right[3]
        s2 = sp * sp
        p = 1.0 / (r2 + s2)
        m = jnp.maximum(1.0 - r2, 0.0)
        q = s2 * p
        w = q * q * q
        pm_ = p * m
        bb = pm_ + (2.0 / 3.0)
        return (w * m) * (w * (pm_ + bb) - bb), dx, dy, dz

    def short_pairs(src, y, y2, shift, init):
        for z in range(4):
            i = y * 4 + z
            cols = [right_data(src, y2 * 4 + z2, shift) for z2 in range(max(z - 1, 0), min(z + 2, 4))]
            for t in range(16):
                lanes = pl.ds(8 * t, 8)
                left = [xi[d, i, lanes, :] for d in range(4)]
                tot = None if init else [acc[d, i, lanes, :] for d in range(3)]
                for right in cols:
                    g, dx, dy, dz = short_weight(left, right)
                    g = g * right[4]
                    add = [g * dx, g * dy, g * dz]
                    tot = add if tot is None else [u + v for u, v in zip(tot, add)]
                for d in range(3):
                    acc[d, i, lanes, :] = tot[d]

    def both_ways(src, y, y2, shift, z_lists, same, init, other):
        for z in range(4):
            i = y * 4 + z
            cols = [(z2, right_data(src, y2 * 4 + z2, shift)) for z2 in z_lists[z]]
            back = {z2: None for z2 in z_lists[z]}
            for t in range(16):
                lanes = pl.ds(8 * t, 8)
                left = [xi[d, i, lanes, :] for d in range(5)]
                tot = None if init else [acc_own[d, i, lanes, :] for d in range(3)]
                for z2, right in cols:
                    g, dx, dy, dz = short_weight(left, right)
                    g = g * (left[4] * right[4])
                    add = [g * dx, g * dy, g * dz]
                    tot = add if tot is None else [u + v for u, v in zip(tot, add)]
                    if not (same and z2 == z):
                        back[z2] = add if back[z2] is None else [u + v for u, v in zip(back[z2], add)]
                for d in range(3):
                    acc_own[d, i, lanes, :] = tot[d]
            for z2, got in back.items():
                if got is not None:
                    for d in range(3):
                        other[d, y2 * 4 + z2] = other[d, y2 * 4 + z2] + got[d]

    ALL_Z = [list(range(max(z - 1, 0), min(z + 2, 4))) for z in range(4)]
    UP_Z = [[z] + ([z + 1] if z < 3 else []) for z in range(4)]

    def own_src(d, row):
        return own_ref[d, pl.ds(row, 1), :]

    def same_row(y, _):
        both_ways(own_src, y, y, None, UP_Z, True, True, acc_j)
        return 0


    def next_row(y, _):
        both_ways(own_src, y, y + 1, None, ALL_Z, False, False, acc_j)
        return 0

    pl.semaphore_wait(barrier, NB + 1)

    halo_up = pltpu.make_async_remote_copy(
        src_ref=own_ref, dst_ref=ext.at[0], send_sem=halo_ss.at[0], recv_sem=halo_rs.at[0],
        device_id={"bead": b, "space": up}, device_id_type=MESH)
    halo_down = pltpu.make_async_remote_copy(
        src_ref=own_ref, dst_ref=ext.at[1], send_sem=halo_ss.at[1], recv_sem=halo_rs.at[1],
        device_id={"bead": b, "space": down}, device_id_type=MESH)
    halo_up.start()
    halo_down.start()

    def to_share(src, dst, ss, rs, c):
        target = share_bead(c)

        @pl.when(target != b)
        def _():
            pltpu.make_async_remote_copy(
                src_ref=src.at[c], dst_ref=dst.at[b], send_sem=ss, recv_sem=rs,
                device_id={"bead": target, "space": s}, device_id_type=MESH).start()

        @pl.when(target == b)
        def _():
            pltpu.make_async_copy(src.at[c], dst.at[b], rs).start()

    def sent_share(src, ss):
        @pl.when(is_share)
        def _():
            pltpu.make_async_copy(src.at[pl.ds(0, 15)], src.at[pl.ds(0, 15)], ss).wait()

        @pl.when(jnp.logical_not(is_share))
        def _():
            pltpu.make_async_copy(src, src, ss).wait()

    def send_early(c, _):
        to_share(early_ref, eb, early_ss, early_rs, c)
        return 0

    lax.fori_loop(0, 16, send_early, 0)
    lax.fori_loop(0, 4, same_row, 0)
    lax.fori_loop(0, 3, next_row, 0)

    def ext_src(k):
        return lambda d, row: ext[k, d, pl.ds(row, 1), :]

    def wait_halo(side):
        pltpu.make_async_remote_copy(
            src_ref=own_ref, dst_ref=ext.at[side], send_sem=halo_ss.at[side], recv_sem=halo_rs.at[side],
            device_id={"bead": b, "space": up}, device_id_type=MESH).wait_recv()

    def both(which):
        side = jnp.where(even, 1 - which, which)
        shift = jnp.where(side == 1, 2.0, -2.0)
        return side, shift

    near_side, near_shift = both(0)
    far_side, far_shift = both(1)

    wait_halo(near_side)

    far_space = jnp.where(even, down, up)
    near_space = jnp.where(even, up, down)
    near_from = jnp.where(even, 0, 2)

    def near_row(n, _):
        y = jnp.where(n < 2, n + near_from, n - 2)
        y2 = jnp.where(n < 2, y, y + 1)
        both_ways(ext_src(near_side), y, y2, near_shift, ALL_Z, False, False, acc_n)
        return 0

    lax.fori_loop(0, 5, near_row, 0)
    for d in range(3):
        react_out[d] = -jnp.sum(acc_n[d], 1)
    react = pltpu.make_async_remote_copy(
        src_ref=react_out, dst_ref=react_in, send_sem=react_ss, recv_sem=react_rs,
        device_id={"bead": b, "space": near_space}, device_id_type=MESH)
    react.start()
    halo_up.wait_send()
    halo_down.wait_send()
    sent_share(early_ref, early_ss)
    react.wait()
    for d in range(3):
        base[d] = react_in[d] - jnp.sum(acc_j[d], 1)

    def mm(a, v):
        return jnp.dot(a, v, preferred_element_type=F32, precision=lax.Precision.HIGHEST)

    wait_halo(far_side)

    def far_y(y, _):
        short_pairs(ext_src(far_side), y, y, far_shift, True)

        def far_row(n, _):
            y2 = y - 1 + 2 * n

            @pl.when((y2 >= 0) & (y2 < 4))
            def _():
                short_pairs(ext_src(far_side), y, y2, far_shift, False)
            return 0

        lax.fori_loop(0, 2, far_row, 0)
        for z in range(4):
            c = y * 4 + z
            rows = [jnp.sum((acc[d, c] * xi[4, c] + acc_own[d, c]).T, 0, keepdims=True) + base[d, pl.ds(c, 1), :]
                    for d in range(3)]
            late_out[c] = pm[c] + kcoef[pl.ds(c, 1), :] * jnp.concatenate(rows, 0)
        for z in range(4):
            to_share(late_out, kb, late_ss, late_rs, y * 4 + z)
        return 0

    lax.fori_loop(0, 4, far_y, 0)

    @pl.when(is_share)
    def _():
        pltpu.make_async_copy(eb, eb, early_rs).wait()
        for d in range(3):
            mixed[d] = mm(table_ref[0:72, :], eb[:, d, :]) + mm(table_ref[72:144, :], eb[:, 3 + d, :])


    my_y = my_cell // 4
    my_z = my_cell % 4
    y_first, y_last = jnp.where(my_y == 3, 1, 0), jnp.where(my_y == 0, 1, 2)
    z_first, z_last = jnp.where(my_z == 3, 1, 0), jnp.where(my_z == 0, 1, 2)
    blocks = (y_last - y_first) * (z_last - z_first)
    far_dst = jnp.where(even, 2, 0)
    near_dst = jnp.where(even, 0, 2)
    my_r = (bz8 // 4) * 4 + bx
    has_own = is_share & (my_y - (bz8 % 4) // 2 >= 0) & (my_y - (bz8 % 4) // 2 < 3) & (
        my_z - bz8 % 2 >= 0) & (my_z - bz8 % 2 < 3)

    def over_blocks(body):
        def outer(by, _):
            def inner(bz, _):
                body(by * 2 + bz, my_y - by, my_z - bz)
                return 0

            return lax.fori_loop(z_first, z_last, inner, 0)

        lax.fori_loop(y_first, y_last, outer, 0)

    @pl.when(is_share)
    def _():
        pltpu.make_async_copy(kb, kb, late_rs).wait()
        for d in range(3):
            cont[:, d, :] = mixed[d, 64:72, :] + mm(table_ref[208:216, :], kb[:, d, :])

        def outside(space, slot):
            def body(q, jy, jz):
                for r in range(PC):
                    pltpu.make_async_remote_copy(
                        src_ref=cont.at[r], dst_ref=cb.at[slot, jy, jz], send_sem=cont_ss, recv_sem=cont_rs.at[slot],
                        device_id={"bead": (r % 4) * 8 + (r // 4) * 4 + q, "space": space}, device_id_type=MESH).start()
            over_blocks(body)

        def inside(q, jy, jz):
            for r in range(PC):
                tb = (r % 4) * 8 + (r // 4) * 4 + q

                @pl.when(tb != b)
                def _():
                    pltpu.make_async_remote_copy(
                        src_ref=cont.at[r], dst_ref=cb.at[1, jy, jz], send_sem=cont_own_ss, recv_sem=cont_rs.at[1],
                        device_id={"bead": tb, "space": s}, device_id_type=MESH).start()

                @pl.when(tb == b)
                def _():
                    pltpu.make_async_copy(cont.at[r], cb.at[1, jy, jz], cont_rs.at[1]).start()

        over_blocks(inside)
        outside(near_space, near_dst)
        outside(far_space, far_dst)
        for d in range(3):
            full = mixed[d, 0:64, :] + mm(table_ref[144:208, :], kb[:, d, :])
            ret[:, d, :] = full[0:32]
            ret[:, 3 + d, :] = full[32:64]

        def send_ret(k, _):
            @pl.when(k != b)
            def _():
                pltpu.make_async_remote_copy(
                    src_ref=ret.at[k], dst_ref=rb.at[my_cell], send_sem=ret_ss, recv_sem=ret_rs,
                    device_id={"bead": k, "space": s}, device_id_type=MESH).start()

            @pl.when(k == b)
            def _():
                pltpu.make_async_copy(ret.at[k], rb.at[my_cell], ret_rs).start()
            return 0

        lax.fori_loop(0, NB, send_ret, 0)

    rhi = bz8 // 4
    q = bz8 % 4
    by = q // 2
    bz = q % 2
    flip = lambda bit, v, top: jnp.where(bit == 1, top - v, v)

    def wait_cont(slot):
        pltpu.make_async_copy(cb.at[slot], cb.at[slot], cont_rs.at[slot]).wait()

    wait_cont(1)
    for iy in range(2):
        for iz in range(2):
            wy = by + iy
            wz = bz + iz
            me = cb[1, wy, wz]
            cell = (2 * by + iy) * 4 + 2 * bz + iz
            xs[0, iy, iz] = spread(2.0 * me[0:1])
            xs[1, iy, iz] = spread(2.0 * (me[1:2] + wy.astype(F32)))
            xs[2, iy, iz] = spread(2.0 * (me[2:3] + wz.astype(F32)))
            xs[3, iy, iz] = spread(own_ref[3, pl.ds(cell, 1), :])
            for d in range(3):
                sacc[d, iy, iz] = jnp.zeros((128, 128), F32)

    Y_PAIRS = ((0, 0), (0, 1), (1, 0), (1, 1), (1, 2))

    def slow_pairs(slot, params, shift):
        def one(n, _):
            fy = jnp.where(n < 2, 0, 1)
            jy = flip(by, jnp.where(n < 2, n, n - 2), 2)
            iy = flip(by, fy, 1)
            js = []
            for jz0 in range(3):
                jz = flip(bz, jz0, 2)
                v = cb[slot, jy, jz]
                row = (by + jy) * 4 + bz + jz
                vals = (2.0 * v[0:1] + shift, 2.0 * (v[1:2] + jy.astype(F32)), 2.0 * (v[2:3] + jz.astype(F32)), params(3, row), params(4, row))
                js.append([jnp.broadcast_to(a, (8, 128)) for a in vals])
            for iz0 in range(2):
                iz = flip(bz, iz0, 1)
                for t in range(16):
                    lanes = pl.ds(8 * t, 8)
                    xa, ya, za, sa = (xs[d, iy, iz, lanes, :] for d in range(4))
                    tot = [sacc[d, iy, iz, lanes, :] for d in range(3)]
                    for jz0 in (range(2) if iz0 == 0 else range(3)):
                        xj, yj, zj, sj, ej = js[jz0]
                        dx = xa - xj
                        dy = ya - yj
                        dz = za - zj
                        r2 = dx * dx + dy * dy + dz * dz
                        sp = sa + sj
                        s2 = sp * sp
                        p = 1.0 / (r2 + s2)
                        m2 = jnp.maximum(1.0 - r2, 0.0)
                        m1 = jnp.maximum(1.0 - 0.25 * r2, 0.0)
                        w = s2 * p
                        w = w * w * w
                        ps = p * (m1 * m1 - m2 * m2)
                        bb = ps + (m1 * (1.0 / 6.0) - m2 * (2.0 / 3.0))
                        g = w * (w * (ps + bb) - bb) * ej
                        tot = [tot[0] + g * dx, tot[1] + g * dy, tot[2] + g * dz]
                    for d in range(3):
                        sacc[d, iy, iz, lanes, :] = tot[d]
            return 0

        lax.fori_loop(0, 5, one, 0)

    slow_pairs(1, own_src, 0.0)
    near_slot = near_side * 2
    far_slot = far_side * 2
    wait_cont(near_slot)
    slow_pairs(near_slot, ext_src(near_side), near_shift)
    wait_cont(far_slot)
    slow_pairs(far_slot, ext_src(far_side), far_shift)

    for iy in range(2):
        for iz in range(2):
            cell = (2 * by + iy) * 4 + 2 * bz + iz
            rows = [jnp.sum(sacc[d, iy, iz].T, 0, keepdims=True) for d in range(3)]
            fb[2 * iy + iz] = e48[pl.ds(cell, 1), :] * jnp.concatenate(rows, 0)

    def x_copy(i):
        other = (bx + 1 + i) % 4
        return pltpu.make_async_remote_copy(
            src_ref=fb, dst_ref=xb.at[bx], send_sem=xb_ss.at[i], recv_sem=xb_rs,
            device_id={"bead": other * 8 + bz8, "space": s}, device_id_type=MESH)

    for i in range(3):
        x_copy(i).start()
    pltpu.make_async_copy(fb, xb.at[bx], xb_rs).start()
    pltpu.make_async_copy(rb, rb, ret_rs).wait()
    for d in range(3):
        nx_ref[0, d] = rb[:, d, :]
        np_ref[0, d] = rb[:, 3 + d, :] * mass[...]
    sent_share(late_out, late_ss)

    def wait_slots(sem, n):
        pltpu.make_async_copy(slots.at[pl.ds(0, n)], slots.at[pl.ds(0, n)], sem).wait()

    for nq in (1, 2, 4):
        @pl.when(is_share & (blocks == nq))
        def _():
            wait_slots(cont_ss, 16 * nq)

        @pl.when(is_share & (blocks == nq) & has_own)
        def _():
            wait_slots(cont_own_ss, 8 * nq - 1)

        @pl.when(is_share & (blocks == nq) & jnp.logical_not(has_own))
        def _():
            wait_slots(cont_own_ss, 8 * nq)

    @pl.when(is_share)
    def _():
        pltpu.make_async_copy(ret.at[pl.ds(0, NB - 1)], ret.at[pl.ds(0, NB - 1)], ret_ss).wait()

    pltpu.make_async_copy(xb, xb, xb_rs).wait()

    def z_copy(i):
        other = (bz8 + i) % 8
        return pltpu.make_async_remote_copy(
            src_ref=zs.at[i], dst_ref=zb.at[bz8], send_sem=zb_ss.at[i], recv_sem=zb_rs,
            device_id={"bead": bx * 8 + other, "space": s}, device_id_type=MESH)

    for i in range(8):
        k = bx * 8 + (bz8 + i) % 8
        part = w_ref[rhi * 4, k] * xb[0]
        for x2 in range(1, 4):
            part = part + w_ref[rhi * 4 + x2, k] * xb[x2]
        zs[i] = part
    for i in range(1, 8):
        z_copy(i).start()
    pltpu.make_async_copy(zs.at[0], zb.at[bz8], zb_rs).start()

    pltpu.make_async_copy(zb, zb, zb_rs).wait()
    slow = []
    for c in range(16):
        blk = (c // 8) * 2 + (c % 4) // 2
        at = (c // 4 % 2) * 2 + c % 2
        slow.append(zb[blk, at] + zb[4 + blk, at])
    for d in range(3):
        np_ref[0, d] = np_ref[0, d] + jnp.concatenate([v[d:d + 1] for v in slow], 0)
    for i in range(3):
        x_copy(i).wait_send()
    for i in range(1, 8):
        z_copy(i).wait_send()


def shards(positions, momenta, noise, atom_types, occupancy, type_sigma, type_eps, type_mass):
    table, weights = bead_tables()
    anywhere = pl.BlockSpec(memory_space=pltpu.HBM)
    vm = pl.BlockSpec(memory_space=pltpu.VMEM)
    out = jax.ShapeDtypeStruct((1, 3, 16, 128), F32)
    V = lambda *shape: pltpu.VMEM(shape, F32)
    S = lambda shape, kind: pltpu.SMEM(shape, kind)
    D = pltpu.SemaphoreType.DMA
    flip = lambda v: jnp.transpose(v, (0, 2, 1, 3))
    nx, pn = pl.pallas_call(
        kernel,
        out_shape=(out, out),
        in_specs=[anywhere] * 10,
        out_specs=(vm, vm),
        scratch_shapes=[
            V(1, 3, 16, 128), V(1, 3, 16, 128), V(1, 3, 16, 128), pltpu.VMEM((16, 128), jnp.int32), V(216, 32),
            S((16,), jnp.int32), S((4,), F32), S((4,), F32), S((4,), F32), S((PC, NB), F32),
            V(5, 16, 128), V(16, 6, 128), V(16, 3, 128), V(16, 128), V(16, 128), V(16, 128), V(64, 3, 128),
            V(3, 16, 128, 128), V(3, 16, 8, 128), V(3, 16, 8, 128), V(3, 16, 128), V(3, 16, 128), V(3, 16, 128),
            V(2, 5, 16, 128), V(5, 16, 128, 128), V(3, 16, 128, 128), V(32, 6, 128), V(32, 3, 128),
            V(16, 3, 128), V(3, 72, 128), V(8, 3, 128), V(32, 6, 128), V(16, 6, 128), V(3, 3, 3, 3, 128),
            V(4, 2, 2, 128, 128), V(3, 2, 2, 128, 128), V(4, 3, 128), V(4, 4, 3, 128), V(8, 4, 3, 128), V(8, 4, 3, 128),
            D((10,)), D((2,)), D((2,)), D, D, D, D, D, D, D((3,)), D, D, D((3,)), D, D((8,)), D, D, D,
        ],
        compiler_params=pltpu.CompilerParams(collective_id=0, has_side_effects=True, vmem_limit_bytes=67043328),
    )(flip(positions), flip(momenta), flip(noise), atom_types, occupancy, type_sigma, type_eps, type_mass,
      jnp.asarray(table), jnp.asarray(weights))
    return flip(nx), flip(pn)


def solution(mesh):
    full = P("bead", "space", None, None)
    placed = (full, full, full, P("space", None), P("space"), P(), P(), P())
    return jax.shard_map(shards, mesh=mesh, in_specs=placed, out_specs=(full, full), check_vma=False)
```

```python
import functools
import math

import jax
import jax.numpy as jnp
import numpy as np
from jax import lax
from jax.experimental import pallas as pl
from jax.experimental.pallas import tpu as pltpu
from jax.sharding import PartitionSpec as P

F32 = jnp.float32
MESH = pl.DeviceIdType.MESH
NB = 32
NS = 16
PC = 8
TIME_STEP = 0.05
INVERSE_TEMP = 32.0
CENTROID_FRICTION = 1.0


def mode_table(n):
    k = np.arange(n)[:, None].astype(np.float64)
    m = np.arange(n)[None, :].astype(np.float64)
    phase = 2.0 * np.pi * k * m / n
    c = np.where(m < n / 2, np.sqrt(2.0 / n) * np.cos(phase), np.sqrt(2.0 / n) * np.sin(phase))
    c = np.where(m == n / 2, np.cos(np.pi * k) / np.sqrt(n), c)
    return np.where(m == 0, 1.0 / np.sqrt(n), c)


def bead_tables():
    c = mode_table(NB)
    n = np.arange(NB)
    freq = 2.0 * (NB / INVERSE_TEMP) * np.sin(np.pi * n / NB)
    gamma = np.where(n == 0, CENTROID_FRICTION, 2.0 * freq)
    c1 = np.exp(-gamma * TIME_STEP)
    kick = np.sqrt((1.0 - c1 * c1) / INVERSE_TEMP)
    cosine = np.cos(freq * TIME_STEP)
    sine = np.sin(freq * TIME_STEP)
    drift = np.where(n == 0, TIME_STEP, sine / np.where(n == 0, 1.0, freq))

    def mix(d):
        return (c * d[None, :]) @ c.T

    pick = np.arange(PC)
    pick = np.where(pick <= PC // 2, pick, pick + NB - PC)
    w = np.sqrt(PC / NB) * mode_table(PC) @ c[:, pick].T
    x_from = (mix(cosine), mix(drift * kick), mix(drift * c1))
    p_from = (mix(-freq * sine), mix(cosine * kick), mix(cosine * c1))
    early_x = np.concatenate([x_from[0], p_from[0], w @ x_from[0]], 0)
    early_n = np.concatenate([x_from[1], p_from[1], w @ x_from[1]], 0)
    late = np.concatenate([x_from[2], p_from[2], w @ x_from[2]], 0)
    table = np.concatenate([early_x, early_n, late], 0).astype(np.float32)
    weights = (w * (0.5 * TIME_STEP * NB / PC)).astype(np.float32)
    return table, weights


def share_bead(cell):
    return (cell // 4) * 8 + 2 + cell % 4


def kernel(pos_in, mom_in, noise_in, types_in, occ_in, sig_in, eps_in, mass_in, table_in, w_in, both_ref,
           pos, mom, noise, types, table_ref, occ, ts_sig, ts_eps, ts_mass, w_ref,
           own_ref, early_ref, pm, kcoef, mass, slots, acc_own, acc_j, acc_n, base, react_out, react_in,
           ext, xi, acc, eb, kb, late_out, mixed, cont, ret, rb, cb, xs, sacc, sacc2, sback, fb, xb, zs, zb,
           in_s, halo_ss, halo_rs, early_ss, early_rs, late_ss, late_rs, cont_ss, cont_own_ss, cont_rs, ret_ss, ret_rs,
           xb_ss, xb_rs, zb_ss, zb_rs, react_ss, react_rs):
    b = lax.axis_index("bead")
    s = lax.axis_index("space")
    bx = b // 8
    nx_ref, np_ref = both_ref.at[0], both_ref.at[1]
    bz8 = b % 8
    up = (s + 1) % NS
    down = (s + NS - 1) % NS
    is_share = (bz8 >= 2) & (bz8 < 6)
    my_cell = bx * 4 + bz8 - 2
    even = s % 2 == 0

    barrier = pltpu.get_barrier_semaphore()

    def greet(i, _):
        other = (b + 1 + i) % NB
        pl.semaphore_signal(barrier, inc=1, device_id={"bead": other, "space": s}, device_id_type=MESH)
        return 0

    pl.semaphore_signal(barrier, inc=1, device_id={"bead": b, "space": up}, device_id_type=MESH)
    pl.semaphore_signal(barrier, inc=1, device_id={"bead": b, "space": down}, device_id_type=MESH)
    lax.fori_loop(0, NB - 1, greet, 0)

    loads = [
        pltpu.make_async_copy(src, dst, in_s.at[i])
        for i, (src, dst) in enumerate((
            (occ_in, occ), (sig_in, ts_sig), (eps_in, ts_eps), (mass_in, ts_mass), (types_in, types),
            (pos_in, pos), (mom_in, mom), (noise_in, noise), (table_in, table_ref), (w_in, w_ref)))
    ]
    for load in loads:
        load.start()
    for load in loads:
        load.wait()

    kind = types[...]

    def pick(tab):
        v = jnp.where(kind == 0, tab[0], tab[1])
        v = jnp.where(kind == 2, tab[2], v)
        return jnp.where(kind == 3, tab[3], v)

    m_all = pick(ts_mass)
    inv = 1.0 / m_all
    slot_index = lax.broadcasted_iota(jnp.int32, (1, 128), 1)
    live = jnp.concatenate([jnp.where(slot_index < occ[c], 1.0, 0.0) for c in range(16)], 0)
    e_all = jnp.sqrt(pick(ts_eps)) * live
    mass[...] = m_all
    kcoef[...] = (0.5 * TIME_STEP * 48.0) * inv
    for d in range(3):
        acc_j[d] = jnp.zeros((16, 8, 128), F32)
        acc_n[d] = jnp.zeros((16, 8, 128), F32)
    root = jnp.sqrt(inv)
    cell_of = lax.broadcasted_iota(jnp.int32, (16, 128), 0)
    corner = (-0.5, (cell_of // 4).astype(F32) - 2.0, (cell_of % 4).astype(F32) - 2.0)
    for d in range(3):
        own_ref[d] = 2.0 * (pos[0, d] + corner[d])
        early_ref[:, d, :] = pos[0, d]
        early_ref[:, 3 + d, :] = noise[0, d] * root
        pm[:, d, :] = mom[0, d] * inv
    own_ref[3] = pick(ts_sig)
    own_ref[4] = e_all

    def spread(ref_row):
        return jnp.broadcast_to(ref_row, (128, 128)).T

    def prep(c, _):
        for d in range(5):
            xi[d, c] = spread(own_ref[d, pl.ds(c, 1), :])
        return 0

    lax.fori_loop(0, 16, prep, 0)

    def right_data(src, row, shift):
        xj = src(0, row)
        if shift is not None:
            xj = xj + shift
        return [jnp.broadcast_to(v, (8, 128)) for v in (xj, src(1, row), src(2, row), src(3, row), src(4, row))]

    def short_weight(left, right):
        dx = left[0] - right[0]
        dy = left[1] - right[1]
        dz = left[2] - right[2]
        r2 = dx * dx + dy * dy + dz * dz
        sp = left[3] + right[3]
        s2 = sp * sp
        p = 1.0 / (r2 + s2)
        m = jnp.maximum(1.0 - r2, 0.0)
        q = s2 * p
        w = q * q * q
        pm_ = p * m
        bb = pm_ + (2.0 / 3.0)
        return (w * m) * (w * (pm_ + bb) - bb), dx, dy, dz

    def short_pairs(src, y, y2, shift, init):
        for z in range(4):
            i = y * 4 + z
            cols = [right_data(src, y2 * 4 + z2, shift) for z2 in range(max(z - 1, 0), min(z + 2, 4))]
            for t in range(16):
                lanes = pl.ds(8 * t, 8)
                left = [xi[d, i, lanes, :] for d in range(4)]
                tot = None if init else [acc[d, i, lanes, :] for d in range(3)]
                for right in cols:
                    g, dx, dy, dz = short_weight(left, right)
                    g = g * right[4]
                    add = [g * dx, g * dy, g * dz]
                    tot = add if tot is None else [u + v for u, v in zip(tot, add)]
                for d in range(3):
                    acc[d, i, lanes, :] = tot[d]

    def both_ways(src, y, y2, shift, z_lists, same, init, other):
        for z in range(4):
            i = y * 4 + z
            cols = [(z2, right_data(src, y2 * 4 + z2, shift)) for z2 in z_lists[z]]
            back = {z2: None for z2 in z_lists[z]}
            for t in range(16):
                lanes = pl.ds(8 * t, 8)
                left = [xi[d, i, lanes, :] for d in range(5)]
                tot = None if init else [acc_own[d, i, lanes, :] for d in range(3)]
                for z2, right in cols:
                    g, dx, dy, dz = short_weight(left, right)
                    g = g * (left[4] * right[4])
                    add = [g * dx, g * dy, g * dz]
                    tot = add if tot is None else [u + v for u, v in zip(tot, add)]
                    if not (same and z2 == z):
                        back[z2] = add if back[z2] is None else [u + v for u, v in zip(back[z2], add)]
                for d in range(3):
                    acc_own[d, i, lanes, :] = tot[d]
            for z2, got in back.items():
                if got is not None:
                    for d in range(3):
                        other[d, y2 * 4 + z2] = other[d, y2 * 4 + z2] + got[d]

    ALL_Z = [list(range(max(z - 1, 0), min(z + 2, 4))) for z in range(4)]
    UP_Z = [[z] + ([z + 1] if z < 3 else []) for z in range(4)]

    def own_src(d, row):
        return own_ref[d, pl.ds(row, 1), :]

    def same_row(y, _):
        both_ways(own_src, y, y, None, UP_Z, True, True, acc_j)
        return 0


    def next_row(y, _):
        both_ways(own_src, y, y + 1, None, ALL_Z, False, False, acc_j)
        return 0

    pl.semaphore_wait(barrier, NB + 1)

    halo_up = pltpu.make_async_remote_copy(
        src_ref=own_ref, dst_ref=ext.at[0], send_sem=halo_ss.at[0], recv_sem=halo_rs.at[0],
        device_id={"bead": b, "space": up}, device_id_type=MESH)
    halo_down = pltpu.make_async_remote_copy(
        src_ref=own_ref, dst_ref=ext.at[1], send_sem=halo_ss.at[1], recv_sem=halo_rs.at[1],
        device_id={"bead": b, "space": down}, device_id_type=MESH)
    halo_up.start()
    halo_down.start()

    def to_share(src, dst, ss, rs, c):
        target = share_bead(c)

        @pl.when(target != b)
        def _():
            pltpu.make_async_remote_copy(
                src_ref=src.at[c], dst_ref=dst.at[b], send_sem=ss, recv_sem=rs,
                device_id={"bead": target, "space": s}, device_id_type=MESH).start()

        @pl.when(target == b)
        def _():
            pltpu.make_async_copy(src.at[c], dst.at[b], rs).start()

    def sent_share(src, ss):
        @pl.when(is_share)
        def _():
            pltpu.make_async_copy(src.at[pl.ds(0, 15)], src.at[pl.ds(0, 15)], ss).wait()

        @pl.when(jnp.logical_not(is_share))
        def _():
            pltpu.make_async_copy(src, src, ss).wait()

    def send_early(c, _):
        to_share(early_ref, eb, early_ss, early_rs, c)
        return 0

    lax.fori_loop(0, 16, send_early, 0)
    lax.fori_loop(0, 4, same_row, 0)
    lax.fori_loop(0, 3, next_row, 0)

    def ext_src(k):
        return lambda d, row: ext[k, d, pl.ds(row, 1), :]

    def wait_halo(side):
        pltpu.make_async_remote_copy(
            src_ref=own_ref, dst_ref=ext.at[side], send_sem=halo_ss.at[side], recv_sem=halo_rs.at[side],
            device_id={"bead": b, "space": up}, device_id_type=MESH).wait_recv()

    def both(which):
        side = jnp.where(even, 1 - which, which)
        shift = jnp.where(side == 1, 2.0, -2.0)
        return side, shift

    near_side, near_shift = both(0)
    far_side, far_shift = both(1)

    wait_halo(near_side)

    far_space = jnp.where(even, down, up)
    near_space = jnp.where(even, up, down)
    near_from = jnp.where(even, 0, 2)

    def near_row(n, _):
        y = jnp.where(n < 2, n + near_from, n - 2)
        y2 = jnp.where(n < 2, y, y + 1)
        both_ways(ext_src(near_side), y, y2, near_shift, ALL_Z, False, False, acc_n)
        return 0

    lax.fori_loop(0, 5, near_row, 0)
    for d in range(3):
        react_out[d] = -jnp.sum(acc_n[d], 1)
    react = pltpu.make_async_remote_copy(
        src_ref=react_out, dst_ref=react_in, send_sem=react_ss, recv_sem=react_rs,
        device_id={"bead": b, "space": near_space}, device_id_type=MESH)
    react.start()
    halo_up.wait_send()
    halo_down.wait_send()
    sent_share(early_ref, early_ss)
    react.wait()
    for d in range(3):
        base[d] = react_in[d] - jnp.sum(acc_j[d], 1)

    def mm(a, v):
        return jnp.dot(a, v, preferred_element_type=F32, precision=lax.Precision.HIGHEST)

    wait_halo(far_side)

    def far_y(y, _):
        short_pairs(ext_src(far_side), y, y, far_shift, True)

        def far_row(n, _):
            y2 = y - 1 + 2 * n

            @pl.when((y2 >= 0) & (y2 < 4))
            def _():
                short_pairs(ext_src(far_side), y, y2, far_shift, False)
            return 0

        lax.fori_loop(0, 2, far_row, 0)
        for z in range(4):
            c = y * 4 + z
            rows = [jnp.sum((acc[d, c] * xi[4, c] + acc_own[d, c]).T, 0, keepdims=True) + base[d, pl.ds(c, 1), :]
                    for d in range(3)]
            late_out[c] = pm[c] + kcoef[pl.ds(c, 1), :] * jnp.concatenate(rows, 0)
        for z in range(4):
            to_share(late_out, kb, late_ss, late_rs, y * 4 + z)
        return 0

    lax.fori_loop(0, 4, far_y, 0)

    @pl.when(is_share)
    def _():
        pltpu.make_async_copy(eb, eb, early_rs).wait()
        for d in range(3):
            mixed[d] = mm(table_ref[0:72, :], eb[:, d, :]) + mm(table_ref[72:144, :], eb[:, 3 + d, :])


    my_y = my_cell // 4
    my_z = my_cell % 4
    y_first, y_last = jnp.where(my_y == 3, 1, 0), jnp.where(my_y == 0, 1, 2)
    z_first, z_last = jnp.where(my_z == 3, 1, 0), jnp.where(my_z == 0, 1, 2)
    blocks = (y_last - y_first) * (z_last - z_first)
    far_dst = jnp.where(even, 2, 0)
    near_dst = jnp.where(even, 0, 2)
    my_r = (bz8 // 4) * 4 + bx
    has_own = is_share & (my_y - (bz8 % 4) // 2 >= 0) & (my_y - (bz8 % 4) // 2 < 3) & (
        my_z - bz8 % 2 >= 0) & (my_z - bz8 % 2 < 3)

    def over_blocks(body):
        def outer(by, _):
            def inner(bz, _):
                body(by * 2 + bz, my_y - by, my_z - bz)
                return 0

            return lax.fori_loop(z_first, z_last, inner, 0)

        lax.fori_loop(y_first, y_last, outer, 0)

    @pl.when(is_share)
    def _():
        pltpu.make_async_copy(kb, kb, late_rs).wait()
        for d in range(3):
            cont[:, d, :] = mixed[d, 64:72, :] + mm(table_ref[208:216, :], kb[:, d, :])

        def outside(space, slot):
            def body(q, jy, jz):
                for r in range(PC):
                    pltpu.make_async_remote_copy(
                        src_ref=cont.at[r], dst_ref=cb.at[slot, jy, jz], send_sem=cont_ss, recv_sem=cont_rs.at[slot],
                        device_id={"bead": (r % 4) * 8 + (r // 4) * 4 + q, "space": space}, device_id_type=MESH).start()
            over_blocks(body)

        def inside(q, jy, jz):
            for r in range(PC):
                tb = (r % 4) * 8 + (r // 4) * 4 + q

                @pl.when(tb != b)
                def _():
                    pltpu.make_async_remote_copy(
                        src_ref=cont.at[r], dst_ref=cb.at[1, jy, jz], send_sem=cont_own_ss, recv_sem=cont_rs.at[1],
                        device_id={"bead": tb, "space": s}, device_id_type=MESH).start()

                @pl.when(tb == b)
                def _():
                    pltpu.make_async_copy(cont.at[r], cb.at[1, jy, jz], cont_rs.at[1]).start()

        over_blocks(inside)
        outside(near_space, near_dst)
        outside(far_space, far_dst)
        for d in range(3):
            full = mixed[d, 0:64, :] + mm(table_ref[144:208, :], kb[:, d, :])
            ret[:, d, :] = full[0:32]
            ret[:, 3 + d, :] = full[32:64]

        def send_ret(k, _):
            @pl.when(k != b)
            def _():
                pltpu.make_async_remote_copy(
                    src_ref=ret.at[k], dst_ref=rb.at[my_cell], send_sem=ret_ss, recv_sem=ret_rs,
                    device_id={"bead": k, "space": s}, device_id_type=MESH).start()

            @pl.when(k == b)
            def _():
                pltpu.make_async_copy(ret.at[k], rb.at[my_cell], ret_rs).start()
            return 0

        lax.fori_loop(0, NB, send_ret, 0)

    rhi = bz8 // 4
    q = bz8 % 4
    by = q // 2
    bz = q % 2
    flip = lambda bit, v, top: jnp.where(bit == 1, top - v, v)

    def wait_cont(slot):
        pltpu.make_async_copy(cb.at[slot], cb.at[slot], cont_rs.at[slot]).wait()

    def block_cell(n):
        return flip(by, n // 2, 1), flip(bz, n % 2, 1)

    wait_cont(1)
    for n in range(4):
        iy, iz = block_cell(n)
        wy = by + iy
        wz = bz + iz
        me = cb[1, wy, wz]
        cell = (2 * by + iy) * 4 + 2 * bz + iz
        xs[0, n] = spread(2.0 * me[0:1])
        xs[1, n] = spread(2.0 * (me[1:2] + wy.astype(F32)))
        xs[2, n] = spread(2.0 * (me[2:3] + wz.astype(F32)))
        xs[3, n] = spread(own_ref[3, pl.ds(cell, 1), :])
        xs[4, n] = spread(own_ref[4, pl.ds(cell, 1), :])

    def window_data(slot, params, shift, jy0, jz0):
        jy = flip(by, jy0, 2)
        jz = flip(bz, jz0, 2)
        v = cb[slot, jy, jz]
        row = (by + jy) * 4 + bz + jz
        vals = (2.0 * v[0:1] + shift, 2.0 * (v[1:2] + jnp.asarray(jy).astype(F32)), 2.0 * (v[2:3] + jnp.asarray(jz).astype(F32)), params(3, row), params(4, row))
        return [jnp.broadcast_to(a, (8, 128)) for a in vals]

    def long_weight(left, right):
        dx = left[0] - right[0]
        dy = left[1] - right[1]
        dz = left[2] - right[2]
        r2 = dx * dx + dy * dy + dz * dz
        sp = left[3] + right[3]
        s2 = sp * sp
        p = 1.0 / (r2 + s2)
        outer = jnp.maximum(4.0 - r2, 0.0)
        inner = jnp.maximum(1.0 - r2, 0.0)
        inner16 = 16.0 * inner
        w = s2 * p
        w = w * w * w
        ps = p * (outer * outer - inner16 * inner)
        bb = ps + (outer - inner16) * (2.0 / 3.0)
        return w * (w * (ps + bb) - bb), dx, dy, dz

    def plus(tot, add):
        return add if tot is None else [u + v for u, v in zip(tot, add)]

    window = {(jy, jz): window_data(1, own_src, 0.0, jy, jz) for jy in range(3) for jz in range(3)}
    for n in range(4):
        sides = [(jy, jz) for jy in range(3) for jz in range(3)
                 if abs(jy - n // 2) <= 1 and abs(jz - n % 2) <= 1]
        single = [j for j in sides if 2 in j or j == (n // 2, n % 2)]
        double = [j for j in sides if 2 not in j and j[0] * 2 + j[1] > n]
        back = {j: None for j in double}
        for t in range(16):
            lanes = pl.ds(8 * t, 8)
            left = [xs[d, n, lanes, :] for d in range(5)]
            tot = tot2 = None
            for j in single:
                g, dx, dy, dz = long_weight(left, window[j])
                g = g * window[j][4]
                tot = plus(tot, [g * dx, g * dy, g * dz])
            for j in double:
                g, dx, dy, dz = long_weight(left, window[j])
                g = g * (left[4] * window[j][4])
                add = [g * dx, g * dy, g * dz]
                tot2 = plus(tot2, add)
                back[j] = plus(back[j], add)
            for d in range(3):
                sacc[d, n, lanes, :] = tot[d]
                if double:
                    sacc2[d, n, lanes, :] = tot2[d]
        for k, j in enumerate(double):
            at = j[0] * 2 + j[1]
            for d in range(3):
                if n == 0:
                    sback[d, at] = back[j][d]
                else:
                    sback[d, at] = sback[d, at] + back[j][d]

    def slow_pairs(slot, params, shift):
        def one(n, _):
            fy = jnp.where(n < 2, 0, 1)
            jy0 = jnp.where(n < 2, n, n - 2)
            js = [window_data(slot, params, shift, jy0, jz0) for jz0 in range(3)]
            for iz0 in range(2):
                at = fy * 2 + iz0
                for t in range(16):
                    lanes = pl.ds(8 * t, 8)
                    left = [xs[d, at, lanes, :] for d in range(4)]
                    tot = [sacc[d, at, lanes, :] for d in range(3)]
                    for jz0 in (range(2) if iz0 == 0 else range(3)):
                        g, dx, dy, dz = long_weight(left, js[jz0])
                        g = g * js[jz0][4]
                        tot = [tot[0] + g * dx, tot[1] + g * dy, tot[2] + g * dz]
                    for d in range(3):
                        sacc[d, at, lanes, :] = tot[d]
            return 0

        lax.fori_loop(0, 5, one, 0)

    near_slot = near_side * 2
    far_slot = far_side * 2
    wait_cont(near_slot)
    slow_pairs(near_slot, ext_src(near_side), near_shift)
    wait_cont(far_slot)
    slow_pairs(far_slot, ext_src(far_side), far_shift)

    for n in range(4):
        iy, iz = block_cell(n)
        rows = []
        for d in range(3):
            lanes = sacc[d, n] * xs[4, n]
            if n < 3:
                lanes = lanes + sacc2[d, n]
            row = jnp.sum(lanes.T, 0, keepdims=True)
            if n > 0:
                row = row - jnp.sum(sback[d, n], 0, keepdims=True)
            rows.append(3.0 * row)
        fb[2 * iy + iz] = jnp.concatenate(rows, 0)

    def x_copy(i):
        other = (bx + 1 + i) % 4
        return pltpu.make_async_remote_copy(
            src_ref=fb, dst_ref=xb.at[bx], send_sem=xb_ss.at[i], recv_sem=xb_rs,
            device_id={"bead": other * 8 + bz8, "space": s}, device_id_type=MESH)

    for i in range(3):
        x_copy(i).start()
    pltpu.make_async_copy(fb, xb.at[bx], xb_rs).start()
    pltpu.make_async_copy(rb, rb, ret_rs).wait()
    for d in range(3):
        nx_ref[0, d] = rb[:, d, :]
        np_ref[0, d] = rb[:, 3 + d, :] * mass[...]
    sent_share(late_out, late_ss)

    def wait_slots(sem, n):
        pltpu.make_async_copy(slots.at[pl.ds(0, n)], slots.at[pl.ds(0, n)], sem).wait()

    for nq in (1, 2, 4):
        @pl.when(is_share & (blocks == nq))
        def _():
            wait_slots(cont_ss, 16 * nq)

        @pl.when(is_share & (blocks == nq) & has_own)
        def _():
            wait_slots(cont_own_ss, 8 * nq - 1)

        @pl.when(is_share & (blocks == nq) & jnp.logical_not(has_own))
        def _():
            wait_slots(cont_own_ss, 8 * nq)

    @pl.when(is_share)
    def _():
        pltpu.make_async_copy(ret.at[pl.ds(0, NB - 1)], ret.at[pl.ds(0, NB - 1)], ret_ss).wait()

    pltpu.make_async_copy(xb, xb, xb_rs).wait()

    def z_copy(i):
        other = (bz8 + i) % 8
        return pltpu.make_async_remote_copy(
            src_ref=zs.at[i], dst_ref=zb.at[bz8], send_sem=zb_ss.at[i], recv_sem=zb_rs,
            device_id={"bead": bx * 8 + other, "space": s}, device_id_type=MESH)

    for i in range(8):
        k = bx * 8 + (bz8 + i) % 8
        part = w_ref[rhi * 4, k] * xb[0]
        for x2 in range(1, 4):
            part = part + w_ref[rhi * 4 + x2, k] * xb[x2]
        zs[i] = part
    for i in range(1, 8):
        z_copy(i).start()
    pltpu.make_async_copy(zs.at[0], zb.at[bz8], zb_rs).start()

    pltpu.make_async_copy(zb, zb, zb_rs).wait()
    slow = []
    for c in range(16):
        blk = (c // 8) * 2 + (c % 4) // 2
        at = (c // 4 % 2) * 2 + c % 2
        slow.append(zb[blk, at] + zb[4 + blk, at])
    for d in range(3):
        np_ref[0, d] = np_ref[0, d] + jnp.concatenate([v[d:d + 1] for v in slow], 0)
    for i in range(3):
        x_copy(i).wait_send()
    for i in range(1, 8):
        z_copy(i).wait_send()


def shards(positions, momenta, noise, atom_types, occupancy, type_sigma, type_eps, type_mass):
    table, weights = bead_tables()
    anywhere = pl.BlockSpec(memory_space=pltpu.HBM)
    vm = pl.BlockSpec(memory_space=pltpu.VMEM)
    out = jax.ShapeDtypeStruct((1, 3, 16, 128), F32)
    V = lambda *shape: pltpu.VMEM(shape, F32)
    S = lambda shape, kind: pltpu.SMEM(shape, kind)
    D = pltpu.SemaphoreType.DMA
    flip = lambda v: jnp.transpose(v, (0, 2, 1, 3))
    both = pl.pallas_call(
        kernel,
        out_shape=jax.ShapeDtypeStruct((2, 1, 3, 16, 128), F32),
        in_specs=[anywhere] * 10,
        out_specs=vm,
        scratch_shapes=[
            V(1, 3, 16, 128), V(1, 3, 16, 128), V(1, 3, 16, 128), pltpu.VMEM((16, 128), jnp.int32), V(216, 32),
            S((16,), jnp.int32), S((4,), F32), S((4,), F32), S((4,), F32), S((PC, NB), F32),
            V(5, 16, 128), V(16, 6, 128), V(16, 3, 128), V(16, 128), V(16, 128), V(64, 3, 128),
            V(3, 16, 128, 128), V(3, 16, 8, 128), V(3, 16, 8, 128), V(3, 16, 128), V(3, 16, 128), V(3, 16, 128),
            V(2, 5, 16, 128), V(5, 16, 128, 128), V(3, 16, 128, 128), V(32, 6, 128), V(32, 3, 128),
            V(16, 3, 128), V(3, 72, 128), V(8, 3, 128), V(32, 6, 128), V(16, 6, 128), V(3, 3, 3, 3, 128),
            V(5, 4, 128, 128), V(3, 4, 128, 128), V(3, 3, 128, 128), V(3, 4, 8, 128), V(4, 3, 128), V(4, 4, 3, 128), V(8, 4, 3, 128), V(8, 4, 3, 128),
            D((10,)), D((2,)), D((2,)), D, D, D, D, D, D, D((3,)), D, D, D((3,)), D, D((8,)), D, D, D,
        ],
        compiler_params=pltpu.CompilerParams(collective_id=0, has_side_effects=True, vmem_limit_bytes=67043328),
    )(flip(positions), flip(momenta), flip(noise), atom_types, occupancy, type_sigma, type_eps, type_mass,
      jnp.asarray(table), jnp.asarray(weights))
    return flip(both[0]), flip(both[1])


def solution(mesh):
    full = P("bead", "space", None, None)
    placed = (full, full, full, P("space", None), P("space"), P(), P(), P())
    return jax.shard_map(shards, mesh=mesh, in_specs=placed, out_specs=(full, full), check_vma=False)
```

```python
import functools
import math

import jax
import jax.numpy as jnp
import numpy as np
from jax import lax
from jax.experimental import pallas as pl
from jax.experimental.pallas import tpu as pltpu
from jax.sharding import PartitionSpec as P

F32 = jnp.float32
MESH = pl.DeviceIdType.MESH
NB = 32
NS = 16
PC = 8
TIME_STEP = 0.05
INVERSE_TEMP = 32.0
CENTROID_FRICTION = 1.0


def mode_table(n):
    k = np.arange(n)[:, None].astype(np.float64)
    m = np.arange(n)[None, :].astype(np.float64)
    phase = 2.0 * np.pi * k * m / n
    c = np.where(m < n / 2, np.sqrt(2.0 / n) * np.cos(phase), np.sqrt(2.0 / n) * np.sin(phase))
    c = np.where(m == n / 2, np.cos(np.pi * k) / np.sqrt(n), c)
    return np.where(m == 0, 1.0 / np.sqrt(n), c)


def bead_tables():
    c = mode_table(NB)
    n = np.arange(NB)
    freq = 2.0 * (NB / INVERSE_TEMP) * np.sin(np.pi * n / NB)
    gamma = np.where(n == 0, CENTROID_FRICTION, 2.0 * freq)
    c1 = np.exp(-gamma * TIME_STEP)
    kick = np.sqrt((1.0 - c1 * c1) / INVERSE_TEMP)
    cosine = np.cos(freq * TIME_STEP)
    sine = np.sin(freq * TIME_STEP)
    drift = np.where(n == 0, TIME_STEP, sine / np.where(n == 0, 1.0, freq))

    def mix(d):
        return (c * d[None, :]) @ c.T

    pick = np.arange(PC)
    pick = np.where(pick <= PC // 2, pick, pick + NB - PC)
    w = np.sqrt(PC / NB) * mode_table(PC) @ c[:, pick].T
    x_from = (mix(cosine), mix(drift * kick), mix(drift * c1))
    p_from = (mix(-freq * sine), mix(cosine * kick), mix(cosine * c1))
    early_x = np.concatenate([x_from[0], p_from[0], w @ x_from[0]], 0)
    early_n = np.concatenate([x_from[1], p_from[1], w @ x_from[1]], 0)
    late = np.concatenate([x_from[2], p_from[2], w @ x_from[2]], 0)
    table = np.concatenate([early_x, early_n, late], 0).astype(np.float32)
    weights = (w * (0.5 * TIME_STEP * NB / PC)).astype(np.float32)
    return table, weights


def share_bead(cell):
    return (cell // 4) * 8 + 2 + cell % 4


def kernel(pos_in, mom_in, noise_in, types_in, occ_in, sig_in, eps_in, mass_in, table_in, w_in, both_ref,
           pos, mom, noise, types, table_ref, occ, ts_sig, ts_eps, ts_mass, w_ref,
           own_ref, early_ref, pm, kcoef, mass, slots, acc_own, acc_j, acc_n, base, react_out, react_in,
           ext, xi, acc, eb, kb, late_out, mixed, cont, ret, rb, cb, xs, sacc, sacc2, sback, fb, xb, zs, zb,
           in_s, halo_ss, halo_rs, early_ss, early_rs, late_ss, late_rs, cont_ss, cont_own_ss, cont_rs, ret_ss, ret_rs,
           xb_ss, xb_rs, zb_ss, zb_rs, react_ss, react_rs):
    b = lax.axis_index("bead")
    s = lax.axis_index("space")
    bx = b // 8
    nx_ref, np_ref = both_ref.at[0], both_ref.at[1]
    bz8 = b % 8
    up = (s + 1) % NS
    down = (s + NS - 1) % NS
    is_share = (bz8 >= 2) & (bz8 < 6)
    my_cell = bx * 4 + bz8 - 2
    even = s % 2 == 0

    barrier = pltpu.get_barrier_semaphore()

    def greet(i, _):
        other = (b + 1 + i) % NB
        pl.semaphore_signal(barrier, inc=1, device_id={"bead": other, "space": s}, device_id_type=MESH)
        return 0

    pl.semaphore_signal(barrier, inc=1, device_id={"bead": b, "space": up}, device_id_type=MESH)
    pl.semaphore_signal(barrier, inc=1, device_id={"bead": b, "space": down}, device_id_type=MESH)
    lax.fori_loop(0, NB - 1, greet, 0)

    loads = [
        pltpu.make_async_copy(src, dst, in_s.at[i])
        for i, (src, dst) in enumerate((
            (occ_in, occ), (sig_in, ts_sig), (eps_in, ts_eps), (mass_in, ts_mass), (types_in, types),
            (pos_in, pos), (mom_in, mom), (noise_in, noise), (table_in, table_ref), (w_in, w_ref)))
    ]
    for load in loads:
        load.start()
    for load in loads:
        load.wait()

    kind = types[...]

    def pick(tab):
        v = jnp.where(kind == 0, tab[0], tab[1])
        v = jnp.where(kind == 2, tab[2], v)
        return jnp.where(kind == 3, tab[3], v)

    m_all = pick(ts_mass)
    inv = 1.0 / m_all
    slot_index = lax.broadcasted_iota(jnp.int32, (1, 128), 1)
    live = jnp.concatenate([jnp.where(slot_index < occ[c], 1.0, 0.0) for c in range(16)], 0)
    e_all = jnp.sqrt(pick(ts_eps)) * live
    mass[...] = m_all
    kcoef[...] = (0.5 * TIME_STEP * 48.0) * inv
    for d in range(3):
        acc_j[d] = jnp.zeros((16, 8, 128), F32)
        acc_n[d] = jnp.zeros((16, 8, 128), F32)
    root = jnp.sqrt(inv)
    cell_of = lax.broadcasted_iota(jnp.int32, (16, 128), 0)
    corner = (-0.5, (cell_of // 4).astype(F32) - 2.0, (cell_of % 4).astype(F32) - 2.0)
    for d in range(3):
        own_ref[d] = 2.0 * (pos[0, d] + corner[d])
        early_ref[:, d, :] = pos[0, d]
        early_ref[:, 3 + d, :] = noise[0, d] * root
        pm[:, d, :] = mom[0, d] * inv
    own_ref[3] = pick(ts_sig)
    own_ref[4] = e_all

    def spread(ref_row):
        return jnp.broadcast_to(ref_row, (128, 128)).T

    def prep(c, _):
        for d in range(5):
            xi[d, c] = spread(own_ref[d, pl.ds(c, 1), :])
        return 0

    lax.fori_loop(0, 16, prep, 0)

    def right_data(src, row, shift):
        xj = src(0, row)
        if shift is not None:
            xj = xj + shift
        return [jnp.broadcast_to(v, (8, 128)) for v in (xj, src(1, row), src(2, row), src(3, row), src(4, row))]

    def short_weight(left, right):
        dx = left[0] - right[0]
        dy = left[1] - right[1]
        dz = left[2] - right[2]
        r2 = dx * dx + dy * dy + dz * dz
        sp = left[3] + right[3]
        s2 = sp * sp
        p = 1.0 / (r2 + s2)
        m = jnp.maximum(1.0 - r2, 0.0)
        q = s2 * p
        w = q * q * q
        pm_ = p * m
        bb = pm_ + (2.0 / 3.0)
        return (w * m) * (w * (pm_ + bb) - bb), dx, dy, dz

    def short_pairs(src, y, y2, shift, init):
        for z in range(4):
            i = y * 4 + z
            cols = [right_data(src, y2 * 4 + z2, shift) for z2 in range(max(z - 1, 0), min(z + 2, 4))]
            for t in range(16):
                lanes = pl.ds(8 * t, 8)
                left = [xi[d, i, lanes, :] for d in range(4)]
                tot = None if init else [acc[d, i, lanes, :] for d in range(3)]
                for right in cols:
                    g, dx, dy, dz = short_weight(left, right)
                    g = g * right[4]
                    add = [g * dx, g * dy, g * dz]
                    tot = add if tot is None else [u + v for u, v in zip(tot, add)]
                for d in range(3):
                    acc[d, i, lanes, :] = tot[d]

    def both_ways(src, y, y2, shift, z_lists, same, init, other):
        for z in range(4):
            i = y * 4 + z
            cols = [(z2, right_data(src, y2 * 4 + z2, shift)) for z2 in z_lists[z]]
            back = {z2: None for z2 in z_lists[z]}
            for t in range(16):
                lanes = pl.ds(8 * t, 8)
                left = [xi[d, i, lanes, :] for d in range(5)]
                tot = None if init else [acc_own[d, i, lanes, :] for d in range(3)]
                for z2, right in cols:
                    g, dx, dy, dz = short_weight(left, right)
                    g = g * (left[4] * right[4])
                    add = [g * dx, g * dy, g * dz]
                    tot = add if tot is None else [u + v for u, v in zip(tot, add)]
                    if not (same and z2 == z):
                        back[z2] = add if back[z2] is None else [u + v for u, v in zip(back[z2], add)]
                for d in range(3):
                    acc_own[d, i, lanes, :] = tot[d]
            for z2, got in back.items():
                if got is not None:
                    for d in range(3):
                        other[d, y2 * 4 + z2] = other[d, y2 * 4 + z2] + got[d]

    ALL_Z = [list(range(max(z - 1, 0), min(z + 2, 4))) for z in range(4)]
    UP_Z = [[z] + ([z + 1] if z < 3 else []) for z in range(4)]

    def own_src(d, row):
        return own_ref[d, pl.ds(row, 1), :]

    def same_row(y, _):
        both_ways(own_src, y, y, None, UP_Z, True, True, acc_j)
        return 0


    def next_row(y, _):
        both_ways(own_src, y, y + 1, None, ALL_Z, False, False, acc_j)
        return 0

    pl.semaphore_wait(barrier, NB + 1)

    def halo(side, part):
        cells = pl.ds(8 * part, 8)
        return pltpu.make_async_remote_copy(
            src_ref=own_ref.at[:, cells, :], dst_ref=ext.at[side, :, cells, :],
            send_sem=halo_ss.at[side, part], recv_sem=halo_rs.at[side, part],
            device_id={"bead": b, "space": jnp.where(side == 0, up, down)}, device_id_type=MESH)

    for part in range(2):
        for side in range(2):
            halo(side, part).start()

    def to_share(src, dst, ss, rs, c):
        target = share_bead(c)

        @pl.when(target != b)
        def _():
            pltpu.make_async_remote_copy(
                src_ref=src.at[c], dst_ref=dst.at[b], send_sem=ss, recv_sem=rs,
                device_id={"bead": target, "space": s}, device_id_type=MESH).start()

        @pl.when(target == b)
        def _():
            pltpu.make_async_copy(src.at[c], dst.at[b], rs).start()

    def sent_share(src, ss):
        @pl.when(is_share)
        def _():
            pltpu.make_async_copy(src.at[pl.ds(0, 15)], src.at[pl.ds(0, 15)], ss).wait()

        @pl.when(jnp.logical_not(is_share))
        def _():
            pltpu.make_async_copy(src, src, ss).wait()

    def send_early(c, _):
        to_share(early_ref, eb, early_ss, early_rs, c)
        return 0

    lax.fori_loop(0, 16, send_early, 0)
    lax.fori_loop(0, 4, same_row, 0)
    lax.fori_loop(0, 3, next_row, 0)

    def ext_src(k):
        return lambda d, row: ext[k, d, pl.ds(row, 1), :]

    def both(which):
        side = jnp.where(even, 1 - which, which)
        shift = jnp.where(side == 1, 2.0, -2.0)
        return side, shift

    near_side, near_shift = both(0)
    far_side, far_shift = both(1)

    halo(near_side, 0).wait_recv()
    halo(near_side, 1).wait_recv()

    far_space = jnp.where(even, down, up)
    near_space = jnp.where(even, up, down)
    near_from = jnp.where(even, 0, 2)

    def near_row(n, _):
        y = jnp.where(n < 2, n + near_from, n - 2)
        y2 = jnp.where(n < 2, y, y + 1)
        both_ways(ext_src(near_side), y, y2, near_shift, ALL_Z, False, False, acc_n)
        return 0

    lax.fori_loop(0, 5, near_row, 0)
    for d in range(3):
        react_out[d] = -jnp.sum(acc_n[d], 1)
    react = pltpu.make_async_remote_copy(
        src_ref=react_out, dst_ref=react_in, send_sem=react_ss, recv_sem=react_rs,
        device_id={"bead": b, "space": near_space}, device_id_type=MESH)
    react.start()
    for part in range(2):
        for side in range(2):
            halo(side, part).wait_send()
    sent_share(early_ref, early_ss)
    react.wait()
    for d in range(3):
        base[d] = react_in[d] - jnp.sum(acc_j[d], 1)

    def mm(a, v):
        return jnp.dot(a, v, preferred_element_type=F32, precision=lax.Precision.HIGHEST)

    halo(far_side, 0).wait_recv()

    def far_y(y, _):
        @pl.when(y == 1)
        def _():
            halo(far_side, 1).wait_recv()

        short_pairs(ext_src(far_side), y, y, far_shift, True)

        def far_row(n, _):
            y2 = y - 1 + 2 * n

            @pl.when((y2 >= 0) & (y2 < 4))
            def _():
                short_pairs(ext_src(far_side), y, y2, far_shift, False)
            return 0

        lax.fori_loop(0, 2, far_row, 0)
        for z in range(4):
            c = y * 4 + z
            rows = [jnp.sum((acc[d, c] * xi[4, c] + acc_own[d, c]).T, 0, keepdims=True) + base[d, pl.ds(c, 1), :]
                    for d in range(3)]
            late_out[c] = pm[c] + kcoef[pl.ds(c, 1), :] * jnp.concatenate(rows, 0)
        for z in range(4):
            to_share(late_out, kb, late_ss, late_rs, y * 4 + z)
        return 0

    lax.fori_loop(0, 4, far_y, 0)

    @pl.when(is_share)
    def _():
        pltpu.make_async_copy(eb, eb, early_rs).wait()
        for d in range(3):
            mixed[d] = mm(table_ref[0:72, :], eb[:, d, :]) + mm(table_ref[72:144, :], eb[:, 3 + d, :])


    my_y = my_cell // 4
    my_z = my_cell % 4
    y_first, y_last = jnp.where(my_y == 3, 1, 0), jnp.where(my_y == 0, 1, 2)
    z_first, z_last = jnp.where(my_z == 3, 1, 0), jnp.where(my_z == 0, 1, 2)
    blocks = (y_last - y_first) * (z_last - z_first)
    far_dst = jnp.where(even, 2, 0)
    near_dst = jnp.where(even, 0, 2)
    my_r = (bz8 // 4) * 4 + bx
    has_own = is_share & (my_y - (bz8 % 4) // 2 >= 0) & (my_y - (bz8 % 4) // 2 < 3) & (
        my_z - bz8 % 2 >= 0) & (my_z - bz8 % 2 < 3)

    def over_blocks(body):
        def outer(by, _):
            def inner(bz, _):
                body(by * 2 + bz, my_y - by, my_z - bz)
                return 0

            return lax.fori_loop(z_first, z_last, inner, 0)

        lax.fori_loop(y_first, y_last, outer, 0)

    @pl.when(is_share)
    def _():
        pltpu.make_async_copy(kb, kb, late_rs).wait()
        for d in range(3):
            cont[:, d, :] = mixed[d, 64:72, :] + mm(table_ref[208:216, :], kb[:, d, :])

        def outside(space, slot):
            def body(q, jy, jz):
                for r in range(PC):
                    pltpu.make_async_remote_copy(
                        src_ref=cont.at[r], dst_ref=cb.at[slot, jy, jz], send_sem=cont_ss, recv_sem=cont_rs.at[slot],
                        device_id={"bead": (r % 4) * 8 + (r // 4) * 4 + q, "space": space}, device_id_type=MESH).start()
            over_blocks(body)

        def inside(q, jy, jz):
            for r in range(PC):
                tb = (r % 4) * 8 + (r // 4) * 4 + q

                @pl.when(tb != b)
                def _():
                    pltpu.make_async_remote_copy(
                        src_ref=cont.at[r], dst_ref=cb.at[1, jy, jz], send_sem=cont_own_ss, recv_sem=cont_rs.at[1],
                        device_id={"bead": tb, "space": s}, device_id_type=MESH).start()

                @pl.when(tb == b)
                def _():
                    pltpu.make_async_copy(cont.at[r], cb.at[1, jy, jz], cont_rs.at[1]).start()

        over_blocks(inside)
        outside(near_space, near_dst)
        outside(far_space, far_dst)
        for d in range(3):
            full = mixed[d, 0:64, :] + mm(table_ref[144:208, :], kb[:, d, :])
            ret[:, d, :] = full[0:32]
            ret[:, 3 + d, :] = full[32:64]

        def send_ret(k, _):
            @pl.when(k != b)
            def _():
                pltpu.make_async_remote_copy(
                    src_ref=ret.at[k], dst_ref=rb.at[my_cell], send_sem=ret_ss, recv_sem=ret_rs,
                    device_id={"bead": k, "space": s}, device_id_type=MESH).start()

            @pl.when(k == b)
            def _():
                pltpu.make_async_copy(ret.at[k], rb.at[my_cell], ret_rs).start()
            return 0

        lax.fori_loop(0, NB, send_ret, 0)

    rhi = bz8 // 4
    q = bz8 % 4
    by = q // 2
    bz = q % 2
    flip = lambda bit, v, top: jnp.where(bit == 1, top - v, v)

    def wait_cont(slot):
        pltpu.make_async_copy(cb.at[slot], cb.at[slot], cont_rs.at[slot]).wait()

    def block_cell(n):
        return flip(by, n // 2, 1), flip(bz, n % 2, 1)

    wait_cont(1)
    for n in range(4):
        iy, iz = block_cell(n)
        wy = by + iy
        wz = bz + iz
        me = cb[1, wy, wz]
        cell = (2 * by + iy) * 4 + 2 * bz + iz
        xs[0, n] = spread(2.0 * me[0:1])
        xs[1, n] = spread(2.0 * (me[1:2] + wy.astype(F32)))
        xs[2, n] = spread(2.0 * (me[2:3] + wz.astype(F32)))
        xs[3, n] = spread(own_ref[3, pl.ds(cell, 1), :])
        xs[4, n] = spread(own_ref[4, pl.ds(cell, 1), :])

    def window_data(slot, params, shift, jy0, jz0):
        jy = flip(by, jy0, 2)
        jz = flip(bz, jz0, 2)
        v = cb[slot, jy, jz]
        row = (by + jy) * 4 + bz + jz
        vals = (2.0 * v[0:1] + shift, 2.0 * (v[1:2] + jnp.asarray(jy).astype(F32)), 2.0 * (v[2:3] + jnp.asarray(jz).astype(F32)), params(3, row), params(4, row))
        return [jnp.broadcast_to(a, (8, 128)) for a in vals]

    def long_weight(left, right):
        dx = left[0] - right[0]
        dy = left[1] - right[1]
        dz = left[2] - right[2]
        r2 = dx * dx + dy * dy + dz * dz
        sp = left[3] + right[3]
        s2 = sp * sp
        p = 1.0 / (r2 + s2)
        outer = jnp.maximum(4.0 - r2, 0.0)
        inner = jnp.maximum(1.0 - r2, 0.0)
        inner16 = 16.0 * inner
        w = s2 * p
        w = w * w * w
        ps = p * (outer * outer - inner16 * inner)
        bb = ps + (outer - inner16) * (2.0 / 3.0)
        return w * (w * (ps + bb) - bb), dx, dy, dz

    def plus(tot, add):
        return add if tot is None else [u + v for u, v in zip(tot, add)]

    window = {(jy, jz): window_data(1, own_src, 0.0, jy, jz) for jy in range(3) for jz in range(3)}
    for n in range(4):
        sides = [(jy, jz) for jy in range(3) for jz in range(3)
                 if abs(jy - n // 2) <= 1 and abs(jz - n % 2) <= 1]
        single = [j for j in sides if 2 in j or j == (n // 2, n % 2)]
        double = [j for j in sides if 2 not in j and j[0] * 2 + j[1] > n]
        back = {j: None for j in double}
        for t in range(16):
            lanes = pl.ds(8 * t, 8)
            left = [xs[d, n, lanes, :] for d in range(5)]
            tot = tot2 = None
            for j in single:
                g, dx, dy, dz = long_weight(left, window[j])
                g = g * window[j][4]
                tot = plus(tot, [g * dx, g * dy, g * dz])
            for j in double:
                g, dx, dy, dz = long_weight(left, window[j])
                g = g * (left[4] * window[j][4])
                add = [g * dx, g * dy, g * dz]
                tot2 = plus(tot2, add)
                back[j] = plus(back[j], add)
            for d in range(3):
                sacc[d, n, lanes, :] = tot[d]
                if double:
                    sacc2[d, n, lanes, :] = tot2[d]
        for k, j in enumerate(double):
            at = j[0] * 2 + j[1]
            for d in range(3):
                if n == 0:
                    sback[d, at] = back[j][d]
                else:
                    sback[d, at] = sback[d, at] + back[j][d]

    def slow_pairs(slot, params, shift):
        def one(n, _):
            fy = jnp.where(n < 2, 0, 1)
            jy0 = jnp.where(n < 2, n, n - 2)
            js = [window_data(slot, params, shift, jy0, jz0) for jz0 in range(3)]
            for iz0 in range(2):
                at = fy * 2 + iz0
                for t in range(16):
                    lanes = pl.ds(8 * t, 8)
                    left = [xs[d, at, lanes, :] for d in range(4)]
                    tot = [sacc[d, at, lanes, :] for d in range(3)]
                    for jz0 in (range(2) if iz0 == 0 else range(3)):
                        g, dx, dy, dz = long_weight(left, js[jz0])
                        g = g * js[jz0][4]
                        tot = [tot[0] + g * dx, tot[1] + g * dy, tot[2] + g * dz]
                    for d in range(3):
                        sacc[d, at, lanes, :] = tot[d]
            return 0

        lax.fori_loop(0, 5, one, 0)

    near_slot = near_side * 2
    far_slot = far_side * 2
    wait_cont(near_slot)
    slow_pairs(near_slot, ext_src(near_side), near_shift)
    wait_cont(far_slot)
    slow_pairs(far_slot, ext_src(far_side), far_shift)

    for n in range(4):
        iy, iz = block_cell(n)
        rows = []
        for d in range(3):
            lanes = sacc[d, n] * xs[4, n]
            if n < 3:
                lanes = lanes + sacc2[d, n]
            row = jnp.sum(lanes.T, 0, keepdims=True)
            if n > 0:
                row = row - jnp.sum(sback[d, n], 0, keepdims=True)
            rows.append(3.0 * row)
        fb[2 * iy + iz] = jnp.concatenate(rows, 0)

    def x_copy(i):
        other = (bx + 1 + i) % 4
        return pltpu.make_async_remote_copy(
            src_ref=fb, dst_ref=xb.at[bx], send_sem=xb_ss.at[i], recv_sem=xb_rs,
            device_id={"bead": other * 8 + bz8, "space": s}, device_id_type=MESH)

    for i in range(3):
        x_copy(i).start()
    pltpu.make_async_copy(fb, xb.at[bx], xb_rs).start()
    pltpu.make_async_copy(rb, rb, ret_rs).wait()
    for d in range(3):
        nx_ref[0, d] = rb[:, d, :]
        np_ref[0, d] = rb[:, 3 + d, :] * mass[...]
    sent_share(late_out, late_ss)

    def wait_slots(sem, n):
        pltpu.make_async_copy(slots.at[pl.ds(0, n)], slots.at[pl.ds(0, n)], sem).wait()

    for nq in (1, 2, 4):
        @pl.when(is_share & (blocks == nq))
        def _():
            wait_slots(cont_ss, 16 * nq)

        @pl.when(is_share & (blocks == nq) & has_own)
        def _():
            wait_slots(cont_own_ss, 8 * nq - 1)

        @pl.when(is_share & (blocks == nq) & jnp.logical_not(has_own))
        def _():
            wait_slots(cont_own_ss, 8 * nq)

    @pl.when(is_share)
    def _():
        pltpu.make_async_copy(ret.at[pl.ds(0, NB - 1)], ret.at[pl.ds(0, NB - 1)], ret_ss).wait()

    pltpu.make_async_copy(xb, xb, xb_rs).wait()

    def z_copy(i):
        other = (bz8 + i) % 8
        return pltpu.make_async_remote_copy(
            src_ref=zs.at[i], dst_ref=zb.at[bz8], send_sem=zb_ss.at[i], recv_sem=zb_rs,
            device_id={"bead": bx * 8 + other, "space": s}, device_id_type=MESH)

    for i in range(8):
        k = bx * 8 + (bz8 + i) % 8
        part = w_ref[rhi * 4, k] * xb[0]
        for x2 in range(1, 4):
            part = part + w_ref[rhi * 4 + x2, k] * xb[x2]
        zs[i] = part
    for i in range(1, 8):
        z_copy(i).start()
    pltpu.make_async_copy(zs.at[0], zb.at[bz8], zb_rs).start()

    pltpu.make_async_copy(zb, zb, zb_rs).wait()
    slow = []
    for c in range(16):
        blk = (c // 8) * 2 + (c % 4) // 2
        at = (c // 4 % 2) * 2 + c % 2
        slow.append(zb[blk, at] + zb[4 + blk, at])
    for d in range(3):
        np_ref[0, d] = np_ref[0, d] + jnp.concatenate([v[d:d + 1] for v in slow], 0)
    for i in range(3):
        x_copy(i).wait_send()
    for i in range(1, 8):
        z_copy(i).wait_send()


def shards(positions, momenta, noise, atom_types, occupancy, type_sigma, type_eps, type_mass):
    table, weights = bead_tables()
    anywhere = pl.BlockSpec(memory_space=pltpu.HBM)
    vm = pl.BlockSpec(memory_space=pltpu.VMEM)
    out = jax.ShapeDtypeStruct((1, 3, 16, 128), F32)
    V = lambda *shape: pltpu.VMEM(shape, F32)
    S = lambda shape, kind: pltpu.SMEM(shape, kind)
    D = pltpu.SemaphoreType.DMA
    flip = lambda v: jnp.transpose(v, (0, 2, 1, 3))
    both = pl.pallas_call(
        kernel,
        out_shape=jax.ShapeDtypeStruct((2, 1, 3, 16, 128), F32),
        in_specs=[anywhere] * 10,
        out_specs=vm,
        scratch_shapes=[
            V(1, 3, 16, 128), V(1, 3, 16, 128), V(1, 3, 16, 128), pltpu.VMEM((16, 128), jnp.int32), V(216, 32),
            S((16,), jnp.int32), S((4,), F32), S((4,), F32), S((4,), F32), S((PC, NB), F32),
            V(5, 16, 128), V(16, 6, 128), V(16, 3, 128), V(16, 128), V(16, 128), V(64, 3, 128),
            V(3, 16, 128, 128), V(3, 16, 8, 128), V(3, 16, 8, 128), V(3, 16, 128), V(3, 16, 128), V(3, 16, 128),
            V(2, 5, 16, 128), V(5, 16, 128, 128), V(3, 16, 128, 128), V(32, 6, 128), V(32, 3, 128),
            V(16, 3, 128), V(3, 72, 128), V(8, 3, 128), V(32, 6, 128), V(16, 6, 128), V(3, 3, 3, 3, 128),
            V(5, 4, 128, 128), V(3, 4, 128, 128), V(3, 3, 128, 128), V(3, 4, 8, 128), V(4, 3, 128), V(4, 4, 3, 128), V(8, 4, 3, 128), V(8, 4, 3, 128),
            D((10,)), D((2, 2)), D((2, 2)), D, D, D, D, D, D, D((3,)), D, D, D((3,)), D, D((8,)), D, D, D,
        ],
        compiler_params=pltpu.CompilerParams(collective_id=0, has_side_effects=True, vmem_limit_bytes=67043328),
    )(flip(positions), flip(momenta), flip(noise), atom_types, occupancy, type_sigma, type_eps, type_mass,
      jnp.asarray(table), jnp.asarray(weights))
    return flip(both[0]), flip(both[1])


def solution(mesh):
    full = P("bead", "space", None, None)
    placed = (full, full, full, P("space", None), P("space"), P(), P(), P())
    return jax.shard_map(shards, mesh=mesh, in_specs=placed, out_specs=(full, full), check_vma=False)
```
